32 devices in a mesh: seq: 2 (over x), tensor: 4 (over y, core), dp: 4 (over z).
Axes of the slice: x: 2, y: 2, z: 4, core: 2. Of those that a mesh axis runs over, the one named last changes fastest.
Arguments:
- inputs: bfloat16 [4, 512, 3584], P('dp', 'seq'), may hold values from -6 to 6
- w_query: bfloat16 [3584, 2048], P(('seq', 'dp'), 'tensor'), may hold values from -0.09375 to 0.09375
- w_key: bfloat16 [3584, 1024], P(('seq', 'dp'), 'tensor'), may hold values from -0.09375 to 0.09375
- w_value: bfloat16 [3584, 1024], P(('seq', 'dp'), 'tensor'), may hold values from -0.09375 to 0.09375
- norm_gain: float32 [3584], replicated, may hold values from 0.1 to 1.9
- attn_grad: bfloat16 [4, 512, 2048], P('dp', 'seq', 'tensor'), may hold values from -200 to 200
Outputs:
- grad_query: float32 [3584, 2048], P(('seq', 'dp'), 'tensor')
- grad_key: float32 [3584, 1024], P(('seq', 'dp'), 'tensor')
- grad_value: float32 [3584, 1024], P(('seq', 'dp'), 'tensor')
- input_grad: bfloat16 [4, 512, 3584], P('dp', 'seq', 'tensor')
The draws below stay inside these ranges and needn't reach their ends.
All inputs are finite; a program needn't handle non-finite values.
Results may differ from the reference program's by a relative error of at most 0.01.
Values may be sent and summed in bfloat16 or wider, within the bound.
A program may use at most 64 MiB of HBM per device.

```python
import math
import jax
import jax.numpy as jnp
from jax import lax

D = 3584
H = 8
KVH = 4
HD = 256
TOK_DEV = 256
LENGTH = 512
WINDOW = 256
EXAMPLES = 4


def draw_attn_grad(key, part):
    split_keys = jax.random.split(jax.random.fold_in(key, 17), 3)
    full_shape = (EXAMPLES, LENGTH, H * HD)
    base_draw = jnp.clip(jax.random.normal(split_keys[0], full_shape, jnp.float32), -4.0, 4.0)
    row_scale = jnp.exp(jax.random.uniform(split_keys[1], (EXAMPLES, LENGTH, 1), jnp.float32, math.log(0.3), math.log(3.0)))
    rising = 1.0 + 2.0 * jnp.arange(LENGTH).astype(jnp.float32)[None, :, None] / (LENGTH - 1)
    col_scale = jnp.exp(jax.random.uniform(split_keys[2], (1, 1, H * HD), jnp.float32, math.log(0.3), math.log(3.0)))
    return (base_draw * row_scale * rising * col_scale).astype(jnp.bfloat16)


def block_scale(key, shape, shards, smallest, top_value):
    def one(axis_at, blocks):
        steps = jax.random.uniform(jax.random.fold_in(jax.random.fold_in(key, 6), axis_at), (blocks,), jnp.float32, smallest / len(shards), top_value / len(shards))
        return jnp.repeat(jnp.exp(steps), shape[axis_at] // blocks).reshape((-1,) + (1,) * (len(shape) - axis_at - 1))

    level = one(*shards[0])
    for cut in shards[1:]:
        level = level * one(*cut)
    return level


def centred(key, dims, scale, bound, cuts=(), kind=jnp.bfloat16):
    entries = scale * jax.random.normal(key, dims, jnp.float32)
    if cuts:
        entries = entries * block_scale(key, dims, cuts, -0.22, 0.18)
    return jnp.clip(entries, -bound, bound).astype(kind)


def setup_inputs(seed: int = 0) -> dict:
    key_of = jax.random.split(jax.random.key(seed), 7)
    return {
        "inputs": centred(key_of[0], (EXAMPLES, LENGTH, D), 1.0, 6.0, ((0, 4), (1, 2))),
        "w_query": centred(key_of[1], (D, H * HD), D ** -0.5, 0.09375, ((0, 8), (1, 4))),
        "w_key": centred(key_of[2], (D, KVH * HD), D ** -0.5, 0.09375, ((0, 8), (1, 4))),
        "w_value": centred(key_of[3], (D, KVH * HD), D ** -0.5, 0.09375, ((0, 8), (1, 4))),
        "norm_gain": jnp.clip(1.0 + 0.18 * jax.random.normal(key_of[4], (D,), jnp.float32), 0.1, 1.9),
        "attn_grad": draw_attn_grad(jax.random.fold_in(key_of[6], 71), 0),
    }


EPSILON = 1e-06
SOFTCAP = 50.0
CLIP_BOUND = 1.0
ROPE_BASE = 10000.0

def angles(positions, head_width):
    frequency = ROPE_BASE ** (-2.0 * jnp.arange(head_width // 2).astype(jnp.float32) / head_width)
    phases = positions.astype(jnp.float32)[:, None] * frequency[None, :]
    return (jnp.cos(phases)[:, None, :], jnp.sin(phases)[:, None, :])

def rotate(vectors, cosine, sine_part, direction):
    half_width = vectors.shape[-1] // 2
    first_half = vectors[..., :half_width]
    second_half = vectors[..., half_width:]
    return jnp.concatenate([first_half * cosine - direction * second_half * sine_part, second_half * cosine + direction * first_half * sine_part], -1)

def attend(queries, key_rows, value_rows, query_pos, key_pos, cotangent):
    query_count, head_count, head_width = queries.shape
    kv_heads = key_rows.shape[1]
    group_size = head_count // kv_heads
    grouped_query = queries.reshape(query_count, kv_heads, group_size, head_width).astype(jnp.float32)
    grouped_cot = cotangent.reshape(query_count, kv_heads, group_size, head_width).astype(jnp.float32)
    key_float = key_rows.astype(jnp.float32)
    value_float = value_rows.astype(jnp.float32)
    inv_scale = 1.0 / math.sqrt(head_width)
    logits = jnp.einsum('tkgd,skd->kgts', grouped_query, key_float) * inv_scale
    squash = jnp.tanh(logits / SOFTCAP)
    allowed = (key_pos[None, :] <= query_pos[:, None]) & (key_pos[None, :] > query_pos[:, None] - WINDOW) & (key_pos[None, :] >= 0)
    exp_terms = jnp.where(allowed, jnp.exp(SOFTCAP * squash), 0.0)
    softmax = exp_terms / lax.optimization_barrier(jnp.sum(exp_terms, -1, keepdims=True))
    probs_low = softmax.astype(jnp.bfloat16).astype(jnp.float32)
    dsoftmax = jnp.einsum('tkgd,skd->kgts', grouped_cot, value_float)
    value_grads = jnp.einsum('kgts,tkgd->skd', probs_low, grouped_cot)
    row_delta = lax.optimization_barrier(jnp.sum(softmax * dsoftmax, -1, keepdims=True))
    dlogits = (softmax * (dsoftmax - row_delta) * (1.0 - squash * squash) * inv_scale).astype(jnp.bfloat16).astype(jnp.float32)
    dquery = jnp.einsum('kgts,skd->tkgd', dlogits, key_float).reshape(query_count, head_count, head_width)
    key_grads = jnp.einsum('kgts,tkgd->skd', dlogits, grouped_query)
    return (dquery, key_grads, value_grads)

def example_terms(inputs_one, w_all, norm_gain, cot_one):
    seq_len = inputs_one.shape[0]
    width_q = H * HD
    width_k = KVH * HD
    widened = inputs_one.astype(jnp.float32)
    inverse_rms = lax.rsqrt(lax.optimization_barrier(jnp.mean(widened * widened, -1)) + EPSILON)
    normed = (widened * inverse_rms[:, None] * norm_gain[None, :]).astype(jnp.bfloat16)
    projected = jnp.dot(normed, w_all, preferred_element_type=jnp.float32)
    positions = jnp.arange(seq_len, dtype=jnp.int32)
    cosine, sine_part = angles(positions, HD)
    rotated_query = rotate(projected[:, :width_q].reshape(seq_len, H, HD), cosine, sine_part, 1.0).astype(jnp.bfloat16)
    rotated_keys = rotate(projected[:, width_q:width_q + width_k].reshape(seq_len, KVH, HD), cosine, sine_part, 1.0).astype(jnp.bfloat16)
    value_rows = projected[:, width_q + width_k:].reshape(seq_len, KVH, HD).astype(jnp.bfloat16)
    block_count = seq_len // TOK_DEV
    query_blocks = rotated_query.reshape(block_count, TOK_DEV, H, HD)
    key_blocks = rotated_keys.reshape(block_count, TOK_DEV, KVH, HD)
    value_blocks = value_rows.reshape(block_count, TOK_DEV, KVH, HD)
    zero_block = jnp.zeros_like(key_blocks[:1])
    key_ext = jnp.concatenate([jnp.concatenate([zero_block, key_blocks[:-1]], 0), key_blocks], 1)
    value_ext = jnp.concatenate([jnp.concatenate([zero_block, value_blocks[:-1]], 0), value_blocks], 1)
    cot_blocks = cot_one.reshape(block_count, TOK_DEV, H * HD)
    block_starts = jnp.arange(block_count, dtype=jnp.int32) * TOK_DEV

    def one_block(block_args):
        query_b, key_b, value_b, cot_b, first_row = block_args
        query_pos = first_row + jnp.arange(TOK_DEV, dtype=jnp.int32)
        key_pos = first_row - TOK_DEV + jnp.arange(2 * TOK_DEV, dtype=jnp.int32)
        return attend(query_b, key_b, value_b, query_pos, key_pos, cot_b)
    dquery, key_ext_grad, value_ext_grad = lax.map(one_block, (query_blocks, key_ext, value_ext, cot_blocks, block_starts))
    zero_grad = jnp.zeros_like(key_ext_grad[:1, :TOK_DEV])
    key_grads = key_ext_grad[:, TOK_DEV:] + jnp.concatenate([key_ext_grad[1:, :TOK_DEV], zero_grad], 0)
    value_grads = value_ext_grad[:, TOK_DEV:] + jnp.concatenate([value_ext_grad[1:, :TOK_DEV], zero_grad], 0)
    dquery = rotate(dquery.reshape(seq_len, H, HD), cosine, sine_part, -1.0)
    key_grads = rotate(key_grads.reshape(seq_len, KVH, HD), cosine, sine_part, -1.0)
    d_out = jnp.concatenate([dquery.reshape(seq_len, width_q), key_grads.reshape(seq_len, width_k), value_grads.reshape(seq_len, width_k)], 1).astype(jnp.bfloat16)
    example_grad = jnp.dot(normed.T, d_out, preferred_element_type=jnp.float32)
    dnormed = lax.dot_general(d_out, w_all, (((1,), (1,)), ((), ())), preferred_element_type=jnp.float32)
    scaled = norm_gain[None, :] * dnormed
    mean_term = lax.optimization_barrier(jnp.mean(widened * scaled, -1, keepdims=True))
    input_grad = (inverse_rms[:, None] * scaled - widened * (inverse_rms ** 3)[:, None] * mean_term).astype(jnp.bfloat16)
    return (example_grad, input_grad)

def reference(inputs, w_query, w_key, w_value, norm_gain, attn_grad):
    width_q = H * HD
    width_k = KVH * HD
    w_all = jnp.concatenate([w_query, w_key, w_value], 1)
    entry_count = D * (H + 2 * KVH) * HD

    def step_example(summed, example_args):
        inputs_one, cot_one = example_args
        example_grad, input_grad = example_terms(inputs_one, w_all, norm_gain, cot_one)
        grad_rms = jnp.sqrt(jnp.sum(example_grad * example_grad) / entry_count + EPSILON)
        factor = CLIP_BOUND / jnp.maximum(grad_rms, CLIP_BOUND)
        return (summed + factor * example_grad, input_grad)
    summed, input_grad = lax.scan(step_example, jnp.zeros((D, w_all.shape[1]), jnp.float32), (inputs, attn_grad))
    return (summed[:, :width_q], summed[:, width_q:width_q + width_k], summed[:, width_q + width_k:], input_grad)
```

```python
import functools
import math

import jax
import jax.numpy as jnp
from jax import lax
from jax.experimental import pallas as pl
from jax.experimental.pallas import tpu as pltpu
from jax.sharding import PartitionSpec as P

D = 3584
H = 8
KVH = 4
HD = 256
WINDOW = 256


EPSILON = 1e-06
SOFTCAP = 50.0
CLIP_BOUND = 1.0
ROPE_BASE = 10000.0


def angles(positions, head_width):
    frequency = ROPE_BASE ** (-2.0 * jnp.arange(head_width // 2).astype(jnp.float32) / head_width)
    phases = positions.astype(jnp.float32)[:, None] * frequency[None, :]
    return (jnp.cos(phases)[:, None, :], jnp.sin(phases)[:, None, :])


MESH = pl.DeviceIdType.MESH


def greet(axes, peers=()):
    barrier = pltpu.get_barrier_semaphore()
    for axis in axes:
        count = lax.axis_size(axis)
        me = lax.axis_index(axis)
        for step in (1, -1):

            @pl.when((me + step >= 0) & (me + step < count))
            def _():
                pl.semaphore_signal(
                    barrier, inc=1, device_id={axis: me + step}, device_id_type=MESH
                )

    for peer in peers:
        pl.semaphore_signal(barrier, inc=1, device_id=peer, device_id_type=MESH)
    near = len(peers)
    for axis in axes:
        me = lax.axis_index(axis)
        near = near + jnp.minimum(me, 1) + jnp.minimum(lax.axis_size(axis) - 1 - me, 1)
    pl.semaphore_wait(barrier, near)


class LineGather:
    def __init__(self, order, part, first, second, low, high, x_ref, out_ref, send_sem, recv_sem):
        self.order = order
        self.part, self.first, self.second = part, first, second
        self.rows = pl.ds(low, high - low)
        self.x_ref, self.out_ref = x_ref, out_ref
        self.send_sem, self.recv_sem = send_sem, recv_sem
        self.me = {axis: lax.axis_index(axis) for axis in (first, second)}
        self.count = {axis: lax.axis_size(axis) for axis in (first, second)}
        self.sends = []

    def slot(self, at):
        return self.out_ref.at[tuple(at[axis] for axis in self.order) + (self.rows,)]

    def copy(self, at, axis, step, own):
        way = (0 if axis == "seq" else 2) + (0 if step == 1 else 1)
        return pltpu.make_async_remote_copy(
            src_ref=self.x_ref.at[self.rows] if own else self.slot(at),
            dst_ref=self.slot(at),
            send_sem=self.send_sem.at[self.part, way, at["seq"], at["dp"]],
            recv_sem=self.recv_sem.at[self.part, at["seq"], at["dp"]],
            device_id={axis: self.me[axis] + step},
            device_id_type=MESH,
        )

    def inside(self, axis, value):
        return (value >= 0) & (value < self.count[axis])

    def send(self, at, axis, step, held, own=False):
        ok = held & self.inside(axis, self.me[axis] + step)

        @pl.when(ok)
        def _():
            self.copy(at, axis, step, own).start()

        self.sends.append((at, axis, step, ok, own))

    def receive(self, at, held):
        @pl.when(held)
        def _():
            self.copy(at, self.first, 1, False).wait_recv()

    def steps(self):
        first, second = self.first, self.second
        here = jnp.bool_(True)
        for axis in (first, second):
            for step in (1, -1):
                self.send(dict(self.me), axis, step, here, True)
        yield
        column = [(dict(self.me), here, True)]
        for hop in range(1, self.count[first]):
            for step in (1, -1):
                at = {**self.me, first: self.me[first] - step * hop}
                held = self.inside(first, at[first])
                self.receive(at, held)
                self.send(at, first, step, held)
                for way in (1, -1):
                    self.send(at, second, way, held)
                column.append((at, held, False))
            yield
        for hop in range(1, self.count[second]):
            for base, held_base, _ in column:
                for step in (1, -1):
                    at = {**base, second: self.me[second] - step * hop}
                    held = held_base & self.inside(second, at[second])
                    self.receive(at, held)
                    self.send(at, second, step, held)
            yield

    def finish(self):
        for at, axis, step, ok, own in self.sends:

            @pl.when(ok)
            def _():
                self.copy(at, axis, step, own).wait_send()


def run_gathers(gathers):
    live = [gather.steps() for gather in gathers]
    while live:
        still = []
        for walk in live:
            try:
                next(walk)
                still.append(walk)
            except StopIteration:
                pass
        live = still
    for gather in gathers:
        gather.finish()


def gather_kernel(cut, order, x_ref, out_ref, send_sem, recv_sem, own_sem):
    rows = x_ref.shape[0]
    own = pltpu.make_async_copy(
        x_ref, out_ref.at[tuple(lax.axis_index(axis) for axis in order)], own_sem
    )
    own.start()
    greet(("seq", "dp"))
    run_gathers(
        [
            LineGather(order, 0, "seq", "dp", 0, cut, x_ref, out_ref, send_sem, recv_sem),
            LineGather(order, 1, "dp", "seq", cut, rows, x_ref, out_ref, send_sem, recv_sem),
        ]
    )
    own.wait()


def gather_blocks(x, cut, order, collective_id):
    shape = (lax.axis_size("seq"), lax.axis_size("dp"))
    return pl.pallas_call(
        functools.partial(gather_kernel, cut, order),
        out_shape=jax.ShapeDtypeStruct(
            tuple(lax.axis_size(axis) for axis in order) + x.shape, x.dtype
        ),
        in_specs=[pl.BlockSpec(memory_space=pltpu.VMEM)],
        out_specs=pl.BlockSpec(memory_space=pl.ANY),
        scratch_shapes=[
            pltpu.SemaphoreType.DMA((2, 4) + shape),
            pltpu.SemaphoreType.DMA((2,) + shape),
            pltpu.SemaphoreType.DMA,
        ],
        compiler_params=pltpu.CompilerParams(
            collective_id=collective_id, has_side_effects=True
        ),
    )(x)


def tail_kernel(
    cut,
    order,
    x_ref,
    part_ref,
    inner_ref,
    block_ref,
    out_ref,
    parts_ref,
    inners_ref,
    blocks_ref,
    send_sem,
    recv_sem,
    own_sem,
    part_send,
    part_recv,
    inner_send,
    inner_recv,
    block_send,
    block_recv,
):
    rows = x_ref.shape[0]
    count, me = lax.axis_size("tensor"), lax.axis_index("tensor")
    width = part_ref.shape[1] // count

    def slab(index):
        return part_ref.at[:, pl.ds(pl.multiple_of(index * width, 128), width)]

    owns = [
        pltpu.make_async_copy(
            x_ref, out_ref.at[tuple(lax.axis_index(axis) for axis in order)], own_sem.at[0]
        ),
        pltpu.make_async_copy(slab(me), parts_ref.at[me], own_sem.at[1]),
        pltpu.make_async_copy(inner_ref, inners_ref.at[me], own_sem.at[2]),
        pltpu.make_async_copy(block_ref, blocks_ref.at[me], own_sem.at[3]),
    ]
    for own in owns:
        own.start()
    others = [lax.rem(me + hop, count) for hop in range(1, count)]
    greet(("seq", "dp"), [{"tensor": other} for other in others])
    copies = []
    for index, other in enumerate(others):
        copies.append(
            pltpu.make_async_remote_copy(
                src_ref=slab(other),
                dst_ref=parts_ref.at[me],
                send_sem=part_send.at[index],
                recv_sem=part_recv.at[index],
                device_id={"tensor": other},
                device_id_type=MESH,
            )
        )
        copies.append(
            pltpu.make_async_remote_copy(
                src_ref=inner_ref,
                dst_ref=inners_ref.at[me],
                send_sem=inner_send.at[index],
                recv_sem=inner_recv.at[index],
                device_id={"tensor": other},
                device_id_type=MESH,
            )
        )
    for index, other in enumerate(others):
        copies.append(
            pltpu.make_async_remote_copy(
                src_ref=block_ref,
                dst_ref=blocks_ref.at[me],
                send_sem=block_send.at[index],
                recv_sem=block_recv.at[index],
                device_id={"tensor": other},
                device_id_type=MESH,
            )
        )
    for copy in copies:
        copy.start()
    run_gathers(
        [
            LineGather(order, 0, "seq", "dp", 0, cut, x_ref, out_ref, send_sem, recv_sem),
            LineGather(order, 1, "dp", "seq", cut, rows, x_ref, out_ref, send_sem, recv_sem),
        ]
    )
    for copy in copies:
        copy.wait()
    for own in owns:
        own.wait()


def gather_and_scatter(x, part, inner, block, cut, order, collective_id):
    shape = (lax.axis_size("seq"), lax.axis_size("dp"))
    count = lax.axis_size("tensor")
    return pl.pallas_call(
        functools.partial(tail_kernel, cut, order),
        out_shape=(
            jax.ShapeDtypeStruct(tuple(lax.axis_size(axis) for axis in order) + x.shape, x.dtype),
            jax.ShapeDtypeStruct((count, part.shape[0], part.shape[1] // count), part.dtype),
            jax.ShapeDtypeStruct((count,) + inner.shape, inner.dtype),
            jax.ShapeDtypeStruct((count,) + block.shape, block.dtype),
        ),
        in_specs=[pl.BlockSpec(memory_space=pltpu.VMEM)] * 4,
        out_specs=(pl.BlockSpec(memory_space=pl.ANY),) * 4,
        scratch_shapes=[
            pltpu.SemaphoreType.DMA((2, 4) + shape),
            pltpu.SemaphoreType.DMA((2,) + shape),
            pltpu.SemaphoreType.DMA((4,)),
        ]
        + [pltpu.SemaphoreType.DMA((count - 1,))] * 6,
        compiler_params=pltpu.CompilerParams(
            collective_id=collective_id, has_side_effects=True
        ),
    )(x, part, inner, block)


def block_peers():
    seqs, dps = lax.axis_size("seq"), lax.axis_size("dp")
    mine = lax.axis_index("dp") * seqs + lax.axis_index("seq")
    others = [lax.rem(mine + hop, seqs * dps) for hop in range(1, seqs * dps)]
    return mine, [(other, lax.rem(other, seqs), other // seqs) for other in others]


def tensor_peers():
    count, me = lax.axis_size("tensor"), lax.axis_index("tensor")
    return [lax.rem(me + hop, count) for hop in range(1, count)]


class Exchange:
    def __init__(self, x_ref, out_ref, send_sem, recv_sem, own_sem):
        self.x_ref, self.out_ref = x_ref, out_ref
        self.send_sem, self.recv_sem, self.own_sem = send_sem, recv_sem, own_sem
        self.lanes, self.lane = lax.axis_size("tensor"), lax.axis_index("tensor")
        self.mine, self.peers = block_peers()
        self.sender = lax.rem(self.mine, self.lanes) == self.lane

    def copy(self, hop, slot):
        _, seq, dp = self.peers[hop]
        return pltpu.make_async_remote_copy(
            src_ref=self.x_ref.at[seq, dp],
            dst_ref=self.out_ref.at[slot],
            send_sem=self.send_sem.at[hop],
            recv_sem=self.recv_sem.at[slot],
            device_id={"seq": seq, "dp": dp},
            device_id_type=MESH,
        )

    def own(self):
        return pltpu.make_async_copy(
            self.x_ref.at[lax.axis_index("seq"), lax.axis_index("dp")],
            self.out_ref.at[self.mine // self.lanes],
            self.own_sem,
        )

    def start(self):
        @pl.when(self.sender)
        def _():
            for hop in range(len(self.peers)):
                self.copy(hop, self.mine // self.lanes).start()
            self.own().start()

    def finish(self):
        for slot in range((len(self.peers) + 1) // self.lanes):

            @pl.when(self.lane + slot * self.lanes != self.mine)
            def _():
                self.copy(0, slot).wait_recv()

        @pl.when(self.sender)
        def _():
            for hop in range(len(self.peers)):
                self.copy(hop, self.mine // self.lanes).wait_send()
            self.own().wait()


def exchange_semaphores():
    count, lanes = lax.axis_size("seq") * lax.axis_size("dp"), lax.axis_size("tensor")
    return [
        pltpu.SemaphoreType.DMA((count - 1,)),
        pltpu.SemaphoreType.DMA((count // lanes,)),
        pltpu.SemaphoreType.DMA,
    ]


def turn(vectors, cosine, sine_part, direction):
    half = vectors.shape[-1] // 2
    low, high = vectors[:, :half], vectors[:, half:]
    return jnp.concatenate(
        [
            low * cosine - direction * high * sine_part,
            high * cosine + direction * low * sine_part,
        ],
        -1,
    )


def product(left, right, left_dim, right_dim):
    return lax.dot_general(
        left, right, (((left_dim,), (right_dim,)), ((), ())), preferred_element_type=jnp.float32
    )


def attend_kernel(
    width_q,
    proj_ref,
    cos_ref,
    sin_ref,
    cot_ref,
    block_ref,
    out_ref,
    blocks_ref,
    held,
    before,
    back_out,
    back_in,
    own_grad,
    kv_sems,
    back_sems,
    *exchange_sems,
):
    rows = proj_ref.shape[0]
    width_k = (proj_ref.shape[1] - width_q) // 2
    heads_k = width_k // HD
    group = width_q // width_k
    inv_scale = 1.0 / math.sqrt(HD)
    seqs, seq = lax.axis_size("seq"), lax.axis_index("seq")
    cosine, sine_part = cos_ref[...], sin_ref[...]
    for head in range(heads_k):
        low = head * HD
        at = slice(low, low + HD)
        keys = proj_ref[:, width_q + low : width_q + low + HD]
        held[:, at] = turn(keys, cosine, sine_part, 1.0).astype(jnp.bfloat16)
        values = proj_ref[:, width_q + width_k + low : width_q + width_k + low + HD]
        held[:, width_k + low : width_k + low + HD] = values.astype(jnp.bfloat16)
    _, peers = block_peers()
    greet((), [{"seq": other, "dp": far} for _, other, far in peers])
    ahead = pltpu.make_async_remote_copy(
        src_ref=held,
        dst_ref=before,
        send_sem=kv_sems.at[0],
        recv_sem=kv_sems.at[1],
        device_id={"seq": seq + 1},
        device_id_type=MESH,
    )
    behind = pltpu.make_async_remote_copy(
        src_ref=back_out,
        dst_ref=back_in,
        send_sem=back_sems.at[0],
        recv_sem=back_sems.at[1],
        device_id={"seq": seq - 1},
        device_id_type=MESH,
    )
    has_next, has_last = seq < seqs - 1, seq > 0

    @pl.when(has_next)
    def _():
        ahead.start()

    exchange = Exchange(block_ref, blocks_ref, *exchange_sems)
    exchange.start()

    queries = []
    for head in range(heads_k * group):
        part = proj_ref[:, head * HD : (head + 1) * HD]
        queries.append(turn(part, cosine, sine_part, 1.0).astype(jnp.bfloat16))

    @pl.when(has_last)
    def _():
        ahead.wait_recv()

    @pl.when(jnp.logical_not(has_last))
    def _():
        before[...] = jnp.zeros_like(before)

    query_at = lax.broadcasted_iota(jnp.int32, (rows, rows), 0)
    key_at = lax.broadcasted_iota(jnp.int32, (rows, rows), 1)
    masks = (
        (key_at > query_at + (rows - WINDOW)) & (seq * rows - rows + key_at >= 0),
        (key_at <= query_at) & (key_at > query_at - WINDOW),
    )
    for head in range(heads_k):
        at = slice(head * HD, (head + 1) * HD)
        at_value = slice(width_k + head * HD, width_k + (head + 1) * HD)
        sides = (before, held)
        key_grads, value_grads = [0.0, 0.0], [0.0, 0.0]
        for member in range(group):
            index = head * group + member
            query = queries[index]
            cot = cot_ref[:, index * HD : (index + 1) * HD]
            squashes, terms, slopes = [], [], []
            for side, mask in zip(sides, masks):
                squash = jnp.tanh(product(query, side[:, at], 1, 1) * inv_scale / SOFTCAP)
                squashes.append(squash)
                terms.append(jnp.where(mask, jnp.exp(SOFTCAP * squash), 0.0))
                slopes.append(product(cot, side[:, at_value], 1, 1))
            total = sum(jnp.sum(term, -1, keepdims=True) for term in terms)
            probs = [term / total for term in terms]
            delta = sum(
                jnp.sum(prob * slope, -1, keepdims=True) for prob, slope in zip(probs, slopes)
            )
            dquery = 0.0
            for which in range(2):
                prob, squash = probs[which], squashes[which]
                dlogits = (
                    prob * (slopes[which] - delta) * (1.0 - squash * squash) * inv_scale
                ).astype(jnp.bfloat16)
                dquery = dquery + product(dlogits, sides[which][:, at], 1, 0)
                key_grads[which] = key_grads[which] + product(dlogits, query, 0, 0)
                value_grads[which] = value_grads[which] + product(
                    prob.astype(jnp.bfloat16), cot, 0, 0
                )
            out_ref[:, index * HD : (index + 1) * HD] = turn(
                dquery, cosine, sine_part, -1.0
            ).astype(jnp.bfloat16)
        back_out[:, at] = key_grads[0].astype(jnp.bfloat16)
        back_out[:, at_value] = value_grads[0].astype(jnp.bfloat16)
        own_grad[:, at] = key_grads[1]
        own_grad[:, at_value] = value_grads[1]

    @pl.when(has_last)
    def _():
        behind.start()

    @pl.when(has_next)
    def _():
        behind.wait_recv()
        own_grad[...] += back_in[...].astype(jnp.float32)

    for head in range(heads_k):
        at = slice(head * HD, (head + 1) * HD)
        out_ref[:, width_q + head * HD : width_q + (head + 1) * HD] = turn(
            own_grad[:, at], cosine, sine_part, -1.0
        ).astype(jnp.bfloat16)
    out_ref[:, width_q + width_k :] = own_grad[:, width_k:].astype(jnp.bfloat16)

    @pl.when(has_next)
    def _():
        ahead.wait_send()

    @pl.when(has_last)
    def _():
        behind.wait_send()

    exchange.finish()


def attend_and_exchange(projected, cosine, sine_part, cotangent, blocks, collective_id):
    rows, width_q = cotangent.shape
    width_k = (projected.shape[1] - width_q) // 2
    return pl.pallas_call(
        functools.partial(attend_kernel, width_q),
        out_shape=(
            jax.ShapeDtypeStruct(projected.shape, jnp.bfloat16),
            jax.ShapeDtypeStruct(
                (blocks.shape[0] * blocks.shape[1] // lax.axis_size("tensor"),)
                + blocks.shape[2:],
                blocks.dtype,
            ),
        ),
        in_specs=[pl.BlockSpec(memory_space=pltpu.VMEM)] * 5,
        out_specs=(pl.BlockSpec(memory_space=pltpu.VMEM), pl.BlockSpec(memory_space=pl.ANY)),
        scratch_shapes=[
            pltpu.VMEM((rows, 2 * width_k), jnp.bfloat16),
            pltpu.VMEM((rows, 2 * width_k), jnp.bfloat16),
            pltpu.VMEM((rows, 2 * width_k), jnp.bfloat16),
            pltpu.VMEM((rows, 2 * width_k), jnp.bfloat16),
            pltpu.VMEM((rows, 2 * width_k), jnp.float32),
            pltpu.SemaphoreType.DMA((2,)),
            pltpu.SemaphoreType.DMA((2,)),
        ]
        + exchange_semaphores(),
        compiler_params=pltpu.CompilerParams(
            collective_id=collective_id, has_side_effects=True
        ),
    )(projected, cosine, sine_part, cotangent, blocks)


def total_kernel(x_ref, out_ref, held, send_sem, recv_sem, send_wide, recv_wide, own_sem):
    mine, peers = block_peers()
    lane = lax.axis_index("tensor")
    others = tensor_peers()
    own = pltpu.make_async_copy(x_ref, held.at[lane, mine], own_sem)
    own.start()
    greet(
        (),
        [{"seq": seq, "dp": dp} for _, seq, dp in peers] + [{"tensor": other} for other in others],
    )
    near = [
        pltpu.make_async_remote_copy(
            src_ref=x_ref,
            dst_ref=held.at[lane, mine],
            send_sem=send_sem.at[hop],
            recv_sem=recv_sem.at[mine],
            device_id={"seq": seq, "dp": dp},
            device_id_type=MESH,
        )
        for hop, (_, seq, dp) in enumerate(peers)
    ]
    for copy in near:
        copy.start()
    for index, seq, dp in peers:
        pltpu.make_async_remote_copy(
            src_ref=x_ref,
            dst_ref=held.at[lane, index],
            send_sem=send_sem.at[0],
            recv_sem=recv_sem.at[index],
            device_id={"seq": seq, "dp": dp},
            device_id_type=MESH,
        ).wait_recv()
    own.wait()
    far = [
        pltpu.make_async_remote_copy(
            src_ref=held.at[lane],
            dst_ref=held.at[lane],
            send_sem=send_wide.at[hop],
            recv_sem=recv_wide.at[hop],
            device_id={"tensor": other},
            device_id_type=MESH,
        )
        for hop, other in enumerate(others)
    ]
    for copy in far:
        copy.start()
    for copy in far:
        copy.wait()
    for copy in near:
        copy.wait_send()
    out_ref[...] = jnp.sum(held[...], (0, 1))


def total_of(x, collective_id):
    count, lanes = lax.axis_size("seq") * lax.axis_size("dp"), lax.axis_size("tensor")
    return pl.pallas_call(
        total_kernel,
        out_shape=jax.ShapeDtypeStruct(x.shape, x.dtype),
        in_specs=[pl.BlockSpec(memory_space=pltpu.VMEM)],
        out_specs=pl.BlockSpec(memory_space=pltpu.VMEM),
        scratch_shapes=[
            pltpu.VMEM((lanes, count) + x.shape, x.dtype),
            pltpu.SemaphoreType.DMA((count - 1,)),
            pltpu.SemaphoreType.DMA((count,)),
            pltpu.SemaphoreType.DMA((lanes - 1,)),
            pltpu.SemaphoreType.DMA((lanes - 1,)),
            pltpu.SemaphoreType.DMA,
        ],
        compiler_params=pltpu.CompilerParams(
            collective_id=collective_id, has_side_effects=True
        ),
    )(x)


def cut_of(rows):
    return max(16, rows // 7 // 16 * 16)


def gathered_local(inputs, w_query, w_key, w_value, norm_gain, attn_grad):
    widened = inputs[0].astype(jnp.float32)
    row_count = widened.shape[0]
    inverse_rms = lax.rsqrt(jnp.mean(widened * widened, -1) + EPSILON)
    normed = (widened * inverse_rms[:, None] * norm_gain[None, :]).astype(jnp.bfloat16)
    width_q = w_query.shape[1]
    width_k = w_key.shape[1]
    local_w = jnp.concatenate([w_query, w_key, w_value], 1)
    seqs, dps = lax.axis_size("seq"), lax.axis_size("dp")
    rows_w = local_w.shape[0]
    full_w = gather_blocks(local_w, cut_of(rows_w), ("seq", "dp"), 0)
    full_w = full_w.reshape(seqs * dps * rows_w, -1)
    projected = jnp.dot(normed, full_w, preferred_element_type=jnp.float32)
    start_row = lax.axis_index("seq") * row_count
    cosine, sine_part = angles(start_row + jnp.arange(row_count, dtype=jnp.int32), HD)
    d_out, passed = attend_and_exchange(
        projected,
        cosine[:, 0],
        sine_part[:, 0],
        attn_grad[0],
        normed.T.reshape(seqs, dps, rows_w, row_count),
        3,
    )
    dnormed = lax.dot_general(
        d_out, full_w, (((1,), (1,)), ((), ())), preferred_element_type=jnp.float32
    )
    inner = jnp.sum(widened * norm_gain[None, :] * dnormed, -1).reshape(-1, 128)
    cotangents, parts, inners, slabs = gather_and_scatter(
        d_out, dnormed.astype(jnp.bfloat16), inner, passed, cut_of(row_count), ("dp", "seq"), 2
    )
    grads = []
    lanes = lax.axis_size("tensor")
    for example in range(dps):
        grads.append(
            sum(
                jnp.dot(
                    slabs[(example * seqs + s) % lanes, (example * seqs + s) // lanes],
                    cotangents[example, s],
                    preferred_element_type=jnp.float32
                )
                for s in range(seqs)
            )
        )
    squares = jnp.stack([jnp.sum(grad * grad) for grad in grads])
    square_sum = total_of(jnp.broadcast_to(squares[:, None], (dps, 128)), 1)[:, 0]
    grad_rms = jnp.sqrt(square_sum / (D * (H + 2 * KVH) * HD) + EPSILON)
    factor = CLIP_BOUND / jnp.maximum(grad_rms, CLIP_BOUND)
    clipped = sum(factor[example] * grads[example] for example in range(dps))
    part_width = D // lax.axis_size("tensor")
    offset = lax.axis_index("tensor") * part_width
    part_grad = jnp.sum(parts.astype(jnp.float32), 0)
    gain_slab = lax.dynamic_slice_in_dim(norm_gain, offset, part_width, 0)
    input_slab = lax.dynamic_slice_in_dim(widened, offset, part_width, 1)
    scaled = gain_slab[None, :] * part_grad
    inner_sum = jnp.sum(inners, 0).reshape(row_count)
    mean_term = (inner_sum / D)[:, None]
    input_grad = (
        inverse_rms[:, None] * scaled
        - input_slab * (inverse_rms * inverse_rms * inverse_rms)[:, None] * mean_term
    )
    return (
        clipped[:, :width_q],
        clipped[:, width_q : width_q + width_k],
        clipped[:, width_q + width_k :],
        input_grad.astype(jnp.bfloat16)[None],
    )


def attend_alone_kernel(
    width_q,
    proj_ref,
    cos_ref,
    sin_ref,
    cot_ref,
    out_ref,
    inner_ref,
    held,
    before,
    back_out,
    back_in,
    own_grad,
    kv_sems,
    back_sems,
):
    rows = proj_ref.shape[0]
    width_k = (proj_ref.shape[1] - width_q) // 2
    heads_k = width_k // HD
    group = width_q // width_k
    inv_scale = 1.0 / math.sqrt(HD)
    seqs, seq = lax.axis_size("seq"), lax.axis_index("seq")
    cosine, sine_part = cos_ref[...], sin_ref[...]
    for head in range(heads_k):
        low = head * HD
        at = slice(low, low + HD)
        keys = proj_ref[:, width_q + low : width_q + low + HD]
        held[:, at] = turn(keys, cosine, sine_part, 1.0).astype(jnp.bfloat16)
        values = proj_ref[:, width_q + width_k + low : width_q + width_k + low + HD]
        held[:, width_k + low : width_k + low + HD] = values.astype(jnp.bfloat16)
    greet(("seq",))
    ahead = pltpu.make_async_remote_copy(
        src_ref=held,
        dst_ref=before,
        send_sem=kv_sems.at[0],
        recv_sem=kv_sems.at[1],
        device_id={"seq": seq + 1},
        device_id_type=MESH,
    )
    behind = pltpu.make_async_remote_copy(
        src_ref=back_out,
        dst_ref=back_in,
        send_sem=back_sems.at[0],
        recv_sem=back_sems.at[1],
        device_id={"seq": seq - 1},
        device_id_type=MESH,
    )
    has_next, has_last = seq < seqs - 1, seq > 0

    @pl.when(has_next)
    def _():
        ahead.start()

    queries = []
    for head in range(heads_k * group):
        part = proj_ref[:, head * HD : (head + 1) * HD]
        queries.append(turn(part, cosine, sine_part, 1.0).astype(jnp.bfloat16))

    @pl.when(has_last)
    def _():
        ahead.wait_recv()

    @pl.when(jnp.logical_not(has_last))
    def _():
        before[...] = jnp.zeros_like(before)

    query_at = lax.broadcasted_iota(jnp.int32, (rows, rows), 0)
    key_at = lax.broadcasted_iota(jnp.int32, (rows, rows), 1)
    masks = (
        (key_at > query_at + (rows - WINDOW)) & (seq * rows - rows + key_at >= 0),
        (key_at <= query_at) & (key_at > query_at - WINDOW),
    )
    for head in range(heads_k):
        at = slice(head * HD, (head + 1) * HD)
        at_value = slice(width_k + head * HD, width_k + (head + 1) * HD)
        sides = (before, held)
        key_grads, value_grads = [0.0, 0.0], [0.0, 0.0]
        for member in range(group):
            index = head * group + member
            query = queries[index]
            cot = cot_ref[:, index * HD : (index + 1) * HD]
            squashes, terms, slopes = [], [], []
            for side, mask in zip(sides, masks):
                squash = jnp.tanh(product(query, side[:, at], 1, 1) * inv_scale / SOFTCAP)
                squashes.append(squash)
                terms.append(jnp.where(mask, jnp.exp(SOFTCAP * squash), 0.0))
                slopes.append(product(cot, side[:, at_value], 1, 1))
            total = sum(jnp.sum(term, -1, keepdims=True) for term in terms)
            probs = [term / total for term in terms]
            delta = sum(
                jnp.sum(prob * slope, -1, keepdims=True) for prob, slope in zip(probs, slopes)
            )
            dquery = 0.0
            for which in range(2):
                prob, squash = probs[which], squashes[which]
                dlogits = (
                    prob * (slopes[which] - delta) * (1.0 - squash * squash) * inv_scale
                ).astype(jnp.bfloat16)
                dquery = dquery + product(dlogits, sides[which][:, at], 1, 0)
                key_grads[which] = key_grads[which] + product(dlogits, query, 0, 0)
                value_grads[which] = value_grads[which] + product(
                    prob.astype(jnp.bfloat16), cot, 0, 0
                )
            out_ref[:, index * HD : (index + 1) * HD] = turn(
                dquery, cosine, sine_part, -1.0
            ).astype(jnp.bfloat16)
        back_out[:, at] = key_grads[0].astype(jnp.bfloat16)
        back_out[:, at_value] = value_grads[0].astype(jnp.bfloat16)
        own_grad[:, at] = key_grads[1]
        own_grad[:, at_value] = value_grads[1]

    @pl.when(has_last)
    def _():
        behind.start()

    @pl.when(has_next)
    def _():
        behind.wait_recv()
        own_grad[...] += back_in[...].astype(jnp.float32)

    for head in range(heads_k):
        at = slice(head * HD, (head + 1) * HD)
        out_ref[:, width_q + head * HD : width_q + (head + 1) * HD] = turn(
            own_grad[:, at], cosine, sine_part, -1.0
        ).astype(jnp.bfloat16)
    out_ref[:, width_q + width_k :] = own_grad[:, width_k:].astype(jnp.bfloat16)

    @pl.when(has_next)
    def _():
        ahead.wait_send()

    @pl.when(has_last)
    def _():
        behind.wait_send()

    inner = 0.0
    for low in range(0, out_ref.shape[1], 128):
        at = slice(low, low + 128)
        inner = inner + out_ref[:, at].astype(jnp.float32) * proj_ref[:, at]
    inner = jnp.broadcast_to(jnp.sum(inner, -1, keepdims=True), (rows, 128))
    inner_ref[...] = inner.T[:8]


def attend_alone(projected, cosine, sine_part, cotangent, collective_id):
    rows, width_q = cotangent.shape
    width_k = (projected.shape[1] - width_q) // 2
    return pl.pallas_call(
        functools.partial(attend_alone_kernel, width_q),
        out_shape=(
            jax.ShapeDtypeStruct(projected.shape, jnp.bfloat16),
            jax.ShapeDtypeStruct((8, rows), jnp.float32),
        ),
        in_specs=[pl.BlockSpec(memory_space=pltpu.VMEM)] * 4,
        out_specs=(pl.BlockSpec(memory_space=pltpu.VMEM),) * 2,
        scratch_shapes=[
            pltpu.VMEM((rows, 2 * width_k), jnp.bfloat16),
            pltpu.VMEM((rows, 2 * width_k), jnp.bfloat16),
            pltpu.VMEM((rows, 2 * width_k), jnp.bfloat16),
            pltpu.VMEM((rows, 2 * width_k), jnp.bfloat16),
            pltpu.VMEM((rows, 2 * width_k), jnp.float32),
            pltpu.SemaphoreType.DMA((2,)),
            pltpu.SemaphoreType.DMA((2,)),
        ],
        compiler_params=pltpu.CompilerParams(
            collective_id=collective_id, has_side_effects=True
        ),
    )(projected, cosine, sine_part, cotangent)


def others_of(axis):
    count, me = lax.axis_size(axis), lax.axis_index(axis)
    return [lax.rem(me + hop, count) for hop in range(1, count)]


def signal_all(peers):
    barrier = pltpu.get_barrier_semaphore()
    for peer in peers:
        pl.semaphore_signal(barrier, inc=1, device_id=peer, device_id_type=MESH)
    return barrier


def remote(src, dst, send_sem, recv_sem, device):
    return pltpu.make_async_remote_copy(
        src_ref=src,
        dst_ref=dst,
        send_sem=send_sem,
        recv_sem=recv_sem,
        device_id=device,
        device_id_type=MESH,
    )


def line(axis, far_first):
    count, me = lax.axis_size(axis), lax.axis_index(axis)
    order = range(count - 1, 0, -1) if far_first else range(1, count)
    found = []
    for index, (hop, step) in enumerate((hop, step) for hop in order for step in (-1, 1)):
        at = me + step * hop
        found.append((index, step, at, (at >= 0) & (at < count)))
    return found


def project_kernel(
    x_ref,
    gain_ref,
    wq_ref,
    wk_ref,
    wv_ref,
    proj_ref,
    w_ref,
    slabs_ref,
    rms_ref,
    turned,
    every,
    natural,
    acc,
    sent,
    got,
    w_send,
    w_recv,
    own_sem,
    x_send,
    x_recv,
    f_send,
    f_recv,
    r_send,
    r_recv,
    s_send,
    s_recv,
):
    seqs, dps, lanes = (lax.axis_size(axis) for axis in ("seq", "dp", "tensor"))
    seq, dp, lane = (lax.axis_index(axis) for axis in ("seq", "dp", "tensor"))
    rows, features = x_ref.shape
    block = wq_ref.shape[0]
    share = block // lanes
    mine = pl.ds(pl.multiple_of(lane * share, 16), share)
    peers = [{axis: other} for axis in ("seq", "dp", "tensor") for other in others_of(axis)]
    barrier = signal_all(peers)
    squares = jnp.zeros((rows, 128), jnp.float32)
    for low in range(0, features, 128):
        part = x_ref[:, low : low + 128].astype(jnp.float32)
        squares = squares + part * part
    inverse = lax.rsqrt(jnp.sum(squares, -1, keepdims=True) / features + EPSILON)
    rms_ref[...] = jnp.broadcast_to(inverse, rms_ref.shape)
    pl.semaphore_wait(barrier, len(peers))

    chunks, base = [], 0
    for ref in (wq_ref, wk_ref, wv_ref):
        chunks.append([(ref, low, base + low) for low in range(0, ref.shape[1], HD)])
        base = base + ref.shape[1]
    chunks = chunks[1] + chunks[2] + chunks[0]

    def w_copy(index, hop, other):
        ref, low, to = chunks[index]
        return remote(
            ref.at[:, low : low + HD],
            w_ref.at[seq, :, to : to + HD],
            w_send.at[hop, index],
            w_recv.at[seq, index],
            {"seq": other},
        )

    owns = []
    for index, (ref, low, to) in enumerate(chunks):
        owns.append(
            pltpu.make_async_copy(
                ref.at[:, low : low + HD], w_ref.at[seq, :, to : to + HD], own_sem.at[index]
            )
        )
        owns[-1].start()
        for hop, other in enumerate(others_of("seq")):
            w_copy(index, hop, other).start()

    for low in range(0, features, 128):
        part = x_ref[:, low : low + 128].astype(jnp.float32)
        part = (part * inverse * gain_ref[:, low : low + 128]).astype(jnp.bfloat16).T
        at = low
        while at < low + 128:
            index = at // block
            end = min(low + 128, (index + 1) * block)
            turned[index // dps, index % dps, at - index * block : end - index * block, :] = part[
                at - low : end - low
            ]
            at = end

    def x_copy(other):
        return remote(
            turned.at[:, other, mine],
            every.at[dp, :, mine],
            x_send.at[other],
            x_recv.at[dp],
            {"dp": other},
        )

    own_x = pltpu.make_async_copy(turned.at[:, dp], every.at[dp], own_sem.at[len(chunks)])
    own_x.start()
    for _, _, other, held in line("dp", True):

        @pl.when(held)
        def _():
            x_copy(other).start()

    def f_copy(source, hop, other):
        return remote(
            every.at[source, :, mine],
            every.at[source, :, mine],
            f_send.at[source, hop],
            f_recv.at[source, lane],
            {"tensor": other},
        )

    def f_arrival(source, other):
        part = every.at[source, :, pl.ds(pl.multiple_of(other * share, 16), share)]
        return remote(
            part, part, f_send.at[source, 0], f_recv.at[source, other], {"tensor": other}
        )

    for _, _, source, held in line("dp", False):

        @pl.when(held)
        def _():
            remote(
                every.at[source, :, mine],
                every.at[source, :, mine],
                x_send.at[source],
                x_recv.at[source],
                {"dp": source},
            ).wait_recv()
            for hop, other in enumerate(others_of("tensor")):
                f_copy(source, hop, other).start()

    def partial(source, index):
        _, _, to = chunks[index]
        weights = w_ref[:, :, to : to + HD].reshape(seqs * block, HD)
        return product(natural[source], weights, 1, 0)

    def turn_back(source):
        natural[source] = every[source].reshape(seqs * block, rows).T

    def r_copy(step, index, which, target):
        way = 0 if step == -1 else 1
        return remote(
            sent.at[index, which],
            got.at[way, index, target],
            r_send.at[index, which],
            r_recv.at[way, index, target],
            {"dp": dp + step},
        )

    def upstream(step):
        return dp < dps - 1 if step == -1 else dp > 0

    def r_arrival(step, index, target):
        way = 0 if step == -1 else 1
        remote(
            got.at[way, index, target],
            got.at[way, index, target],
            r_send.at[index, 0],
            r_recv.at[way, index, target],
            {"dp": dp},
        ).wait_recv()
        acc[...] += got[way, index, target].astype(jnp.float32)

    def finish_chunk(index):
        _, _, to = chunks[index]
        acc[...] = partial(dp, index)
        for step in (-1, 1):

            @pl.when(upstream(step))
            def _():
                r_arrival(step, index, dp)

        proj_ref[:, to : to + HD] = acc[...]

    slab_own = pltpu.make_async_copy(
        every.at[:, seq], slabs_ref.at[seq], own_sem.at[len(chunks) + 1]
    )

    def s_copy(hop, other):
        return remote(
            every.at[:, other], slabs_ref.at[seq], s_send.at[hop], s_recv.at[seq], {"seq": other}
        )

    for index in range(len(chunks)):
        owns[index].wait()
        for other in others_of("seq"):
            _, _, to = chunks[index]
            remote(
                w_ref.at[other, :, to : to + HD],
                w_ref.at[other, :, to : to + HD],
                w_send.at[0, index],
                w_recv.at[other, index],
                {"seq": other},
            ).wait_recv()
        for which, step, target, held in line("dp", True):

            @pl.when(held)
            def _():
                if index == 0:
                    for other in others_of("tensor"):
                        f_arrival(target, other).wait_recv()
                    turn_back(target)
                acc[...] = partial(target, index)

                @pl.when(upstream(step))
                def _():
                    r_arrival(step, index, target)

                sent[index, which] = acc[...].astype(jnp.bfloat16)
                r_copy(step, index, which, target).start()

        if index == 0:
            own_x.wait()
            turn_back(dp)
            slab_own.start()
            for hop, other in enumerate(others_of("seq")):
                s_copy(hop, other).start()
        else:
            finish_chunk(index - 1)
    finish_chunk(len(chunks) - 1)

    slab_own.wait()
    for hop, other in enumerate(others_of("seq")):
        s_copy(hop, other).wait_send()
        remote(
            every.at[:, other], slabs_ref.at[other], s_send.at[hop], s_recv.at[other], {"seq": other}
        ).wait_recv()
        for index in range(len(chunks)):
            w_copy(index, hop, other).wait_send()
    for which, step, target, held in line("dp", True):

        @pl.when(held)
        def _():
            x_copy(target).wait_send()
            for hop, other in enumerate(others_of("tensor")):
                f_copy(target, hop, other).wait_send()
            for index in range(len(chunks)):
                r_copy(step, index, which, target).wait_send()


def project(x, gain, w_query, w_key, w_value, collective_id):
    seqs, dps, lanes = (lax.axis_size(axis) for axis in ("seq", "dp", "tensor"))
    rows, features = x.shape
    block = w_query.shape[0]
    width = w_query.shape[1] + w_key.shape[1] + w_value.shape[1]
    count = width // HD
    hops = 2 * (dps - 1)
    vmem = pl.BlockSpec(memory_space=pltpu.VMEM)
    dma = pltpu.SemaphoreType.DMA
    return pl.pallas_call(
        project_kernel,
        out_shape=(
            jax.ShapeDtypeStruct((rows, width), jnp.float32),
            jax.ShapeDtypeStruct((seqs, block, width), jnp.bfloat16),
            jax.ShapeDtypeStruct((seqs, dps, block, rows), jnp.bfloat16),
            jax.ShapeDtypeStruct((rows, 128), jnp.float32),
        ),
        in_specs=[vmem, vmem] + [pl.BlockSpec(memory_space=pl.ANY)] * 3,
        out_specs=(vmem,) * 4,
        scratch_shapes=[
            pltpu.VMEM((seqs, dps, block, rows), jnp.bfloat16),
            pltpu.VMEM((dps, seqs, block, rows), jnp.bfloat16),
            pltpu.VMEM((dps, rows, seqs * block), jnp.bfloat16),
            pltpu.VMEM((rows, HD), jnp.float32),
            pltpu.VMEM((count, hops, rows, HD), jnp.bfloat16),
            pltpu.VMEM((2, count, dps, rows, HD), jnp.bfloat16),
            dma((seqs - 1, count)),
            dma((seqs, count)),
            dma((count + 2,)),
            dma((dps,)),
            dma((dps,)),
            dma((dps, lanes - 1)),
            dma((dps, lanes)),
            dma((count, hops)),
            dma((2, count, dps)),
            dma((seqs - 1,)),
            dma((seqs,)),
        ],
        compiler_params=pltpu.CompilerParams(
            collective_id=collective_id, has_side_effects=True
        ),
    )(x, gain, w_query, w_key, w_value)


def split_rows(rows):
    return max(16, rows // 6 // 16 * 16)


def backward_kernel(
    cut,
    d_out_ref,
    w_ref,
    slabs_ref,
    inner_ref,
    rms_ref,
    x_ref,
    gain_ref,
    gq_ref,
    gk_ref,
    gv_ref,
    out_ref,
    every,
    grads,
    final,
    inners,
    squares,
    small,
    held_sums,
    x_slab,
    *rest,
):
    seqs, dps, lanes = (lax.axis_size(axis) for axis in ("seq", "dp", "tensor"))
    seq, dp, lane = (lax.axis_index(axis) for axis in ("seq", "dp", "tensor"))
    stages = lanes.bit_length() - 1
    parts, rest = rest[: stages + 1], rest[stages + 1 :]
    arrived, rest = rest[:stages], rest[stages:]
    (g_send, g_recv, own_sem, p_send, p_recv, z_send, z_recv, i_send, i_recv) = rest[:9]
    t_send, t_recv, u_send, u_recv = rest[9:]
    rows, width = d_out_ref.shape
    block = w_ref.shape[1]
    per_slab = seqs * dps // lanes
    part_width = per_slab * block
    column_blocks = width // HD

    near = [{"dp": far, "tensor": other} for far in others_of("dp") for other in others_of("tensor")]
    near = near + [{"tensor": other} for other in others_of("tensor")]
    mine, blocks = block_peers()
    near = near + [{"seq": other, "dp": far} for _, other, far in blocks]
    barrier = signal_all(near)
    owns = [
        pltpu.make_async_copy(d_out_ref, every.at[dp, seq], own_sem.at[0]),
        pltpu.make_async_copy(
            x_ref.at[:, pl.ds(pl.multiple_of(lane * part_width, 128), part_width)],
            x_slab,
            own_sem.at[1],
        ),
        pltpu.make_async_copy(inner_ref, inners.at[lane], own_sem.at[2]),
    ]
    for own in owns:
        own.start()
    pl.semaphore_wait(barrier, len(near))

    order = ("dp", "seq")
    by_seq = LineGather(order, 0, "seq", "dp", 0, cut, d_out_ref, every, g_send, g_recv)
    by_dp = LineGather(order, 1, "dp", "seq", cut, rows, d_out_ref, every, g_send, g_recv)
    me = {"seq": seq, "dp": dp}
    here = jnp.bool_(True)
    for gather, axis in ((by_dp, "dp"), (by_dp, "seq"), (by_seq, "seq"), (by_seq, "dp")):
        for step in (1, -1):
            gather.send(dict(me), axis, step, here, True)
    inner_copies = [
        remote(inner_ref, inners.at[lane], i_send.at[hop], i_recv.at[lane], {"tensor": other})
        for hop, other in enumerate(others_of("tensor"))
    ]
    for copy in inner_copies:
        copy.start()

    def weight_grad(at, first):
        def column(index, carry):
            columns = pl.ds(pl.multiple_of(index * HD, HD), HD)
            term = product(slabs_ref[at["seq"], at["dp"]], every[at["dp"], at["seq"], :, columns], 1, 0)
            if first:
                grads[at["dp"], :, columns] = term
            else:
                grads[at["dp"], :, columns] = grads[at["dp"], :, columns] + term
            return carry

        lax.fori_loop(0, column_blocks, column, 0)

    def square_sum(example):
        def some(index, total):
            group = grads[example, pl.ds(pl.multiple_of(index * 16, 16), 16), :]
            group = group * group
            group = group[:8] + group[8:]
            for low in range(0, width, 128):
                total = total + group[:, low : low + 128]
            return total

        total = lax.fori_loop(0, block // 16, some, jnp.zeros((8, 128), jnp.float32))
        squares[example] = total

    bits = [lax.rem(lane // (1 << stage), 2) for stage in range(stages)]
    sizes = [block >> stage for stage in range(stages + 1)]
    start = 0
    for stage in range(stages):
        start = start + bits[stage] * sizes[stage + 1]

    def half(stage, bit):
        return pl.ds(pl.multiple_of(bit * sizes[stage + 1], 16), sizes[stage + 1])

    def p_copy(stage, example):
        return remote(
            parts[stage].at[example, :, half(stage, 1 - bits[stage])],
            arrived[stage].at[example],
            p_send.at[stage, example],
            p_recv.at[stage, example],
            {"tensor": lane + (1 - 2 * bits[stage]) * (1 << stage)},
        )

    def z_target(part):
        index = part * dps + dp
        return index // per_slab, lax.rem(index, per_slab)

    def z_copy(example, part):
        to, slot = z_target(part)
        return remote(
            parts[stages].at[example, part],
            final.at[slot, pl.ds(pl.multiple_of(start, 16), sizes[stages])],
            z_send.at[example, part],
            z_recv.at[slot, lane],
            {"tensor": to, "dp": example},
        )

    def z_own(example, part):
        _, slot = z_target(part)
        return pltpu.make_async_copy(
            parts[stages].at[example, part],
            final.at[slot, pl.ds(pl.multiple_of(start, 16), sizes[stages])],
            z_recv.at[slot, lane],
        )

    def z_is_own(example, part):
        to, _ = z_target(part)
        return (to == lane) & (example == dp)

    def advance(stage, example):
        if stage == 0:
            for part in range(seqs):
                parts[0][example, part] = product(
                    w_ref[part], every[example, seq], 1, 1
                ).astype(jnp.bfloat16)
        else:
            p_copy(stage - 1, example).wait_recv()
            kept = parts[stage - 1][example, :, half(stage - 1, bits[stage - 1])]
            added = arrived[stage - 1][example]
            parts[stage][example] = (
                kept.astype(jnp.float32) + added.astype(jnp.float32)
            ).astype(jnp.bfloat16)
        if stage < stages:
            p_copy(stage, example).start()
        else:
            for part in range(seqs):

                @pl.when(z_is_own(example, part))
                def _():
                    z_own(example, part).start()

                @pl.when(jnp.logical_not(z_is_own(example, part)))
                def _():
                    z_copy(example, part).start()

    groups = [[(dp, None)]] + [
        [
            (dp - step * hop, (dp - step * hop >= 0) & (dp - step * hop < dps))
            for step in (1, -1)
        ]
        for hop in range(1, dps)
    ]

    def each(hop, action):
        for example, held in groups[hop]:
            if held is None:
                action(example)
            else:

                @pl.when(held)
                def _():
                    action(example)

    def spread(hop):
        column = []
        for example, held in groups[hop]:
            column.append(({**me, "dp": example}, here if held is None else held))
        found = []
        for base, held_base in column:
            for far in range(1, seqs):
                for step in (1, -1):
                    at = {**base, "seq": seq - step * far}
                    held = held_base & by_dp.inside("seq", at["seq"])
                    by_dp.receive(at, held)
                    by_dp.send(at, "seq", step, held)
                    found.append((at, held))
        for at, held in found:

            @pl.when(held)
            def _():
                weight_grad(at, False)

        each(hop, square_sum)

    base_columns = [(dict(me), here)]
    for hop in range(1, seqs):
        for step in (1, -1):
            at = {**me, "seq": seq - step * hop}
            held = by_seq.inside("seq", at["seq"])
            by_seq.receive(at, held)
            by_seq.send(at, "seq", step, held)
            for way in (1, -1):
                by_seq.send(at, "dp", way, held)
            base_columns.append((at, held))
    owns[0].wait()
    each(0, functools.partial(advance, 0))
    each(0, lambda example: weight_grad({**me, "dp": example}, True))
    for hop in range(1, dps):
        for step in (1, -1):
            at = {**me, "dp": dp - step * hop}
            held = by_dp.inside("dp", at["dp"])
            by_dp.receive(at, held)
            by_dp.send(at, "dp", step, held)
            for way in (1, -1):
                by_dp.send(at, "seq", way, held)
        for base, held_base in base_columns:
            for step in (1, -1):
                at = {**base, "dp": dp - step * hop}
                held = held_base & by_seq.inside("dp", at["dp"])
                by_seq.receive(at, held)
                by_seq.send(at, "dp", step, held)
        each(hop, functools.partial(advance, 0))
        for stage in range(1, stages + 1):
            if 0 <= hop - stage:
                each(hop - stage, functools.partial(advance, stage))
        each(hop, lambda example: weight_grad({**me, "dp": example}, True))
        spread(hop - 1)
    for late in range(1, stages + 1):
        for stage in range(late, stages + 1):
            if 0 <= dps - 1 + late - stage < dps:
                each(dps - 1 + late - stage, functools.partial(advance, stage))
        if late == 1:
            spread(dps - 1)
            for example in range(dps):
                small[example : example + 1, :] = jnp.sum(squares[example], 0, keepdims=True)
            own_sum = pltpu.make_async_copy(small, held_sums.at[lane, mine], own_sem.at[3])
            own_sum.start()
            sums = [
                remote(
                    small,
                    held_sums.at[lane, mine],
                    t_send.at[hop],
                    t_recv.at[mine],
                    {"seq": other, "dp": far},
                )
                for hop, (_, other, far) in enumerate(blocks)
            ]
            for copy in sums:
                copy.start()

    for hop, (index, other, far) in enumerate(blocks):
        remote(
            small,
            held_sums.at[lane, index],
            t_send.at[hop],
            t_recv.at[index],
            {"seq": other, "dp": far},
        ).wait_recv()
    own_sum.wait()
    wide = [
        remote(
            held_sums.at[lane],
            held_sums.at[lane],
            u_send.at[hop],
            u_recv.at[lane],
            {"tensor": other},
        )
        for hop, other in enumerate(others_of("tensor"))
    ]
    for copy in wide:
        copy.start()

    owns[1].wait()
    owns[2].wait()
    for hop, other in enumerate(others_of("tensor")):
        remote(
            inner_ref, inners.at[other], i_send.at[hop], i_recv.at[other], {"tensor": other}
        ).wait_recv()
    total = inners[0]
    for other in range(1, lanes):
        total = total + inners[other]
    total = jnp.broadcast_to(total[:1], (128, rows)).T
    inverse = rms_ref[...]
    mean = total * inverse * inverse / x_ref.shape[1]
    for slot in range(per_slab):
        for other in range(lanes):
            where, turn_start = other, 0
            for stage in range(stages):
                turn_start = turn_start + (where >> stage) % 2 * sizes[stage + 1]
            piece = final.at[slot, turn_start : turn_start + sizes[stages]]
            remote(
                piece, piece, z_send.at[0, 0], z_recv.at[slot, other], {"tensor": lane}
            ).wait_recv()
    for low in range(0, part_width, 128):
        pieces = []
        at = low
        while at < low + 128:
            slot = at // block
            end = min(low + 128, (slot + 1) * block)
            pieces.append(final[slot, at - slot * block : end - slot * block, :])
            at = end
        part = pieces[0] if len(pieces) == 1 else jnp.concatenate(pieces, 0)
        part = part.astype(jnp.float32).T
        gain = gain_ref[:, pl.ds(pl.multiple_of(lane * part_width + low, 128), 128)]
        scaled = part * gain
        out_ref[:, low : low + 128] = (
            inverse * scaled - x_slab[:, low : low + 128].astype(jnp.float32) * mean
        ).astype(jnp.bfloat16)

    for hop, other in enumerate(others_of("tensor")):
        remote(
            held_sums.at[other],
            held_sums.at[other],
            u_send.at[hop],
            u_recv.at[other],
            {"tensor": other},
        ).wait_recv()
    square = jnp.sum(jnp.sum(held_sums[...], (0, 1)), -1, keepdims=True)
    grad_rms = jnp.sqrt(square / (D * (H + 2 * KVH) * HD) + EPSILON)
    factor = CLIP_BOUND / jnp.maximum(grad_rms, CLIP_BOUND)
    base = 0
    for ref in (gq_ref, gk_ref, gv_ref):
        for low in range(0, ref.shape[1], 128):
            clipped = factor[0:1] * grads[0, :, base + low : base + low + 128]
            for example in range(1, dps):
                clipped = clipped + factor[example : example + 1] * (
                    grads[example, :, base + low : base + low + 128]
                )
            ref[:, low : low + 128] = clipped
        base = base + ref.shape[1]

    by_seq.finish()
    by_dp.finish()
    for copy in inner_copies + sums + wide:
        copy.wait_send()

    def drain(example):
        for stage in range(stages):
            p_copy(stage, example).wait_send()
        for part in range(seqs):

            @pl.when(jnp.logical_not(z_is_own(example, part)))
            def _():
                z_copy(example, part).wait_send()

    for hop in range(dps):
        each(hop, drain)


def backward(d_out, weights, slabs, inner, rms, x, gain, widths, collective_id):
    seqs, dps, lanes = (lax.axis_size(axis) for axis in ("seq", "dp", "tensor"))
    rows, width = d_out.shape
    block = weights.shape[1]
    features = x.shape[1]
    stages = lanes.bit_length() - 1
    per_slab = seqs * dps // lanes
    vmem = pl.BlockSpec(memory_space=pltpu.VMEM)
    dma = pltpu.SemaphoreType.DMA
    count = seqs * dps
    return pl.pallas_call(
        functools.partial(backward_kernel, split_rows(rows)),
        out_shape=tuple(jax.ShapeDtypeStruct((block, size), jnp.float32) for size in widths)
        + (jax.ShapeDtypeStruct((rows, features // lanes), jnp.bfloat16),),
        in_specs=[vmem] * 5 + [pl.BlockSpec(memory_space=pl.ANY), vmem],
        out_specs=(vmem,) * 4,
        scratch_shapes=[
            pltpu.VMEM((dps, seqs, rows, width), jnp.bfloat16),
            pltpu.VMEM((dps, block, width), jnp.float32),
            pltpu.VMEM((per_slab, block, rows), jnp.bfloat16),
            pltpu.VMEM((lanes,) + inner.shape, jnp.float32),
            pltpu.VMEM((dps, 8, 128), jnp.float32),
            pltpu.VMEM((dps, 128), jnp.float32),
            pltpu.VMEM((lanes, count, dps, 128), jnp.float32),
            pltpu.VMEM((rows, features // lanes), jnp.bfloat16),
        ]
        + [
            pltpu.VMEM((dps, seqs, block >> stage, rows), jnp.bfloat16)
            for stage in range(stages + 1)
        ]
        + [
            pltpu.VMEM((dps, seqs, block >> (stage + 1), rows), jnp.bfloat16)
            for stage in range(stages)
        ]
        + [
            dma((2, 4, seqs, dps)),
            dma((2, seqs, dps)),
            dma((4,)),
            dma((stages, dps)),
            dma((stages, dps)),
            dma((dps, seqs)),
            dma((per_slab, lanes)),
            dma((lanes - 1,)),
            dma((lanes,)),
            dma((count - 1,)),
            dma((count,)),
            dma((lanes - 1,)),
            dma((lanes,)),
        ],
        compiler_params=pltpu.CompilerParams(
            collective_id=collective_id, has_side_effects=True
        ),
    )(d_out, weights, slabs, inner, rms, x, gain)


def split_local(inputs, w_query, w_key, w_value, norm_gain, attn_grad):
    x, gain = inputs[0], norm_gain[None, :]
    rows = x.shape[0]
    projected, weights, slabs, rms = project(x, gain, w_query, w_key, w_value, 0)
    start_row = lax.axis_index("seq") * rows
    cosine, sine_part = angles(start_row + jnp.arange(rows, dtype=jnp.int32), HD)
    d_out, inner = attend_alone(projected, cosine[:, 0], sine_part[:, 0], attn_grad[0], 3)
    widths = (w_query.shape[1], w_key.shape[1], w_value.shape[1])
    grad_query, grad_key, grad_value, input_grad = backward(
        d_out, weights, slabs, inner, rms, x, gain, widths, 2
    )
    return grad_query, grad_key, grad_value, input_grad[None]


def local(*args):
    inputs, w_query = args[:2]
    seqs, dps, lanes = (lax.axis_size(axis) for axis in ("seq", "dp", "tensor"))
    block = w_query.shape[0]
    aligned = block % (16 * lanes) == 0 and inputs.shape[1] % 128 == 0
    aligned = aligned and (block * seqs * dps // lanes) % 128 == 0
    even = lanes & (lanes - 1) == 0 and seqs * dps % lanes == 0
    if aligned and even and min(seqs, dps, lanes) > 1:
        return split_local(*args)
    return gathered_local(*args)


def solution(mesh):
    return jax.shard_map(
        local,
        mesh=mesh,
        in_specs=(
            P("dp", "seq", None),
            P(("seq", "dp"), "tensor"),
            P(("seq", "dp"), "tensor"),
            P(("seq", "dp"), "tensor"),
            P(),
            P("dp", "seq", "tensor"),
        ),
        out_specs=(
            P(("seq", "dp"), "tensor"),
            P(("seq", "dp"), "tensor"),
            P(("seq", "dp"), "tensor"),
            P("dp", "seq", "tensor"),
        ),
        check_vma=False,
    )
```

```python
import functools
import math

import jax
import jax.numpy as jnp
from jax import lax
from jax.experimental import pallas as pl
from jax.experimental.pallas import tpu as pltpu
from jax.sharding import PartitionSpec as P

D = 3584
H = 8
KVH = 4
HD = 256
WINDOW = 256


EPSILON = 1e-06
SOFTCAP = 50.0
CLIP_BOUND = 1.0
ROPE_BASE = 10000.0


def angles(positions, head_width):
    frequency = ROPE_BASE ** (-2.0 * jnp.arange(head_width // 2).astype(jnp.float32) / head_width)
    phases = positions.astype(jnp.float32)[:, None] * frequency[None, :]
    return (jnp.cos(phases)[:, None, :], jnp.sin(phases)[:, None, :])


MESH = pl.DeviceIdType.MESH


def greet(axes, peers=()):
    barrier = pltpu.get_barrier_semaphore()
    for axis in axes:
        count = lax.axis_size(axis)
        me = lax.axis_index(axis)
        for step in (1, -1):

            @pl.when((me + step >= 0) & (me + step < count))
            def _():
                pl.semaphore_signal(
                    barrier, inc=1, device_id={axis: me + step}, device_id_type=MESH
                )

    for peer in peers:
        pl.semaphore_signal(barrier, inc=1, device_id=peer, device_id_type=MESH)
    near = len(peers)
    for axis in axes:
        me = lax.axis_index(axis)
        near = near + jnp.minimum(me, 1) + jnp.minimum(lax.axis_size(axis) - 1 - me, 1)
    pl.semaphore_wait(barrier, near)


class LineGather:
    def __init__(self, order, part, first, second, low, high, x_ref, out_ref, send_sem, recv_sem):
        self.order = order
        self.part, self.first, self.second = part, first, second
        self.rows = pl.ds(low, high - low)
        self.x_ref, self.out_ref = x_ref, out_ref
        self.send_sem, self.recv_sem = send_sem, recv_sem
        self.me = {axis: lax.axis_index(axis) for axis in (first, second)}
        self.count = {axis: lax.axis_size(axis) for axis in (first, second)}
        self.sends = []

    def slot(self, at):
        return self.out_ref.at[tuple(at[axis] for axis in self.order) + (self.rows,)]

    def copy(self, at, axis, step, own):
        way = (0 if axis == "seq" else 2) + (0 if step == 1 else 1)
        return pltpu.make_async_remote_copy(
            src_ref=self.x_ref.at[self.rows] if own else self.slot(at),
            dst_ref=self.slot(at),
            send_sem=self.send_sem.at[self.part, way, at["seq"], at["dp"]],
            recv_sem=self.recv_sem.at[self.part, at["seq"], at["dp"]],
            device_id={axis: self.me[axis] + step},
            device_id_type=MESH,
        )

    def inside(self, axis, value):
        return (value >= 0) & (value < self.count[axis])

    def send(self, at, axis, step, held, own=False):
        ok = held & self.inside(axis, self.me[axis] + step)

        @pl.when(ok)
        def _():
            self.copy(at, axis, step, own).start()

        self.sends.append((at, axis, step, ok, own))

    def receive(self, at, held):
        @pl.when(held)
        def _():
            self.copy(at, self.first, 1, False).wait_recv()

    def steps(self):
        first, second = self.first, self.second
        here = jnp.bool_(True)
        for axis in (first, second):
            for step in (1, -1):
                self.send(dict(self.me), axis, step, here, True)
        yield
        column = [(dict(self.me), here, True)]
        for hop in range(1, self.count[first]):
            for step in (1, -1):
                at = {**self.me, first: self.me[first] - step * hop}
                held = self.inside(first, at[first])
                self.receive(at, held)
                self.send(at, first, step, held)
                for way in (1, -1):
                    self.send(at, second, way, held)
                column.append((at, held, False))
            yield
        for hop in range(1, self.count[second]):
            for base, held_base, _ in column:
                for step in (1, -1):
                    at = {**base, second: self.me[second] - step * hop}
                    held = held_base & self.inside(second, at[second])
                    self.receive(at, held)
                    self.send(at, second, step, held)
            yield

    def finish(self):
        for at, axis, step, ok, own in self.sends:

            @pl.when(ok)
            def _():
                self.copy(at, axis, step, own).wait_send()


def run_gathers(gathers):
    live = [gather.steps() for gather in gathers]
    while live:
        still = []
        for walk in live:
            try:
                next(walk)
                still.append(walk)
            except StopIteration:
                pass
        live = still
    for gather in gathers:
        gather.finish()


def gather_kernel(cut, order, x_ref, out_ref, send_sem, recv_sem, own_sem):
    rows = x_ref.shape[0]
    own = pltpu.make_async_copy(
        x_ref, out_ref.at[tuple(lax.axis_index(axis) for axis in order)], own_sem
    )
    own.start()
    greet(("seq", "dp"))
    run_gathers(
        [
            LineGather(order, 0, "seq", "dp", 0, cut, x_ref, out_ref, send_sem, recv_sem),
            LineGather(order, 1, "dp", "seq", cut, rows, x_ref, out_ref, send_sem, recv_sem),
        ]
    )
    own.wait()


def gather_blocks(x, cut, order, collective_id):
    shape = (lax.axis_size("seq"), lax.axis_size("dp"))
    return pl.pallas_call(
        functools.partial(gather_kernel, cut, order),
        out_shape=jax.ShapeDtypeStruct(
            tuple(lax.axis_size(axis) for axis in order) + x.shape, x.dtype
        ),
        in_specs=[pl.BlockSpec(memory_space=pltpu.VMEM)],
        out_specs=pl.BlockSpec(memory_space=pl.ANY),
        scratch_shapes=[
            pltpu.SemaphoreType.DMA((2, 4) + shape),
            pltpu.SemaphoreType.DMA((2,) + shape),
            pltpu.SemaphoreType.DMA,
        ],
        compiler_params=pltpu.CompilerParams(
            collective_id=collective_id, has_side_effects=True
        ),
    )(x)


def tail_kernel(
    cut,
    order,
    x_ref,
    part_ref,
    inner_ref,
    block_ref,
    out_ref,
    parts_ref,
    inners_ref,
    blocks_ref,
    send_sem,
    recv_sem,
    own_sem,
    part_send,
    part_recv,
    inner_send,
    inner_recv,
    block_send,
    block_recv,
):
    rows = x_ref.shape[0]
    count, me = lax.axis_size("tensor"), lax.axis_index("tensor")
    width = part_ref.shape[1] // count

    def slab(index):
        return part_ref.at[:, pl.ds(pl.multiple_of(index * width, 128), width)]

    owns = [
        pltpu.make_async_copy(
            x_ref, out_ref.at[tuple(lax.axis_index(axis) for axis in order)], own_sem.at[0]
        ),
        pltpu.make_async_copy(slab(me), parts_ref.at[me], own_sem.at[1]),
        pltpu.make_async_copy(inner_ref, inners_ref.at[me], own_sem.at[2]),
        pltpu.make_async_copy(block_ref, blocks_ref.at[me], own_sem.at[3]),
    ]
    for own in owns:
        own.start()
    others = [lax.rem(me + hop, count) for hop in range(1, count)]
    greet(("seq", "dp"), [{"tensor": other} for other in others])
    copies = []
    for index, other in enumerate(others):
        copies.append(
            pltpu.make_async_remote_copy(
                src_ref=slab(other),
                dst_ref=parts_ref.at[me],
                send_sem=part_send.at[index],
                recv_sem=part_recv.at[index],
                device_id={"tensor": other},
                device_id_type=MESH,
            )
        )
        copies.append(
            pltpu.make_async_remote_copy(
                src_ref=inner_ref,
                dst_ref=inners_ref.at[me],
                send_sem=inner_send.at[index],
                recv_sem=inner_recv.at[index],
                device_id={"tensor": other},
                device_id_type=MESH,
            )
        )
    for index, other in enumerate(others):
        copies.append(
            pltpu.make_async_remote_copy(
                src_ref=block_ref,
                dst_ref=blocks_ref.at[me],
                send_sem=block_send.at[index],
                recv_sem=block_recv.at[index],
                device_id={"tensor": other},
                device_id_type=MESH,
            )
        )
    for copy in copies:
        copy.start()
    run_gathers(
        [
            LineGather(order, 0, "seq", "dp", 0, cut, x_ref, out_ref, send_sem, recv_sem),
            LineGather(order, 1, "dp", "seq", cut, rows, x_ref, out_ref, send_sem, recv_sem),
        ]
    )
    for copy in copies:
        copy.wait()
    for own in owns:
        own.wait()


def gather_and_scatter(x, part, inner, block, cut, order, collective_id):
    shape = (lax.axis_size("seq"), lax.axis_size("dp"))
    count = lax.axis_size("tensor")
    return pl.pallas_call(
        functools.partial(tail_kernel, cut, order),
        out_shape=(
            jax.ShapeDtypeStruct(tuple(lax.axis_size(axis) for axis in order) + x.shape, x.dtype),
            jax.ShapeDtypeStruct((count, part.shape[0], part.shape[1] // count), part.dtype),
            jax.ShapeDtypeStruct((count,) + inner.shape, inner.dtype),
            jax.ShapeDtypeStruct((count,) + block.shape, block.dtype),
        ),
        in_specs=[pl.BlockSpec(memory_space=pltpu.VMEM)] * 4,
        out_specs=(pl.BlockSpec(memory_space=pl.ANY),) * 4,
        scratch_shapes=[
            pltpu.SemaphoreType.DMA((2, 4) + shape),
            pltpu.SemaphoreType.DMA((2,) + shape),
            pltpu.SemaphoreType.DMA((4,)),
        ]
        + [pltpu.SemaphoreType.DMA((count - 1,))] * 6,
        compiler_params=pltpu.CompilerParams(
            collective_id=collective_id, has_side_effects=True
        ),
    )(x, part, inner, block)


def block_peers():
    seqs, dps = lax.axis_size("seq"), lax.axis_size("dp")
    mine = lax.axis_index("dp") * seqs + lax.axis_index("seq")
    others = [lax.rem(mine + hop, seqs * dps) for hop in range(1, seqs * dps)]
    return mine, [(other, lax.rem(other, seqs), other // seqs) for other in others]


def tensor_peers():
    count, me = lax.axis_size("tensor"), lax.axis_index("tensor")
    return [lax.rem(me + hop, count) for hop in range(1, count)]


class Exchange:
    def __init__(self, x_ref, out_ref, send_sem, recv_sem, own_sem):
        self.x_ref, self.out_ref = x_ref, out_ref
        self.send_sem, self.recv_sem, self.own_sem = send_sem, recv_sem, own_sem
        self.lanes, self.lane = lax.axis_size("tensor"), lax.axis_index("tensor")
        self.mine, self.peers = block_peers()
        self.sender = lax.rem(self.mine, self.lanes) == self.lane

    def copy(self, hop, slot):
        _, seq, dp = self.peers[hop]
        return pltpu.make_async_remote_copy(
            src_ref=self.x_ref.at[seq, dp],
            dst_ref=self.out_ref.at[slot],
            send_sem=self.send_sem.at[hop],
            recv_sem=self.recv_sem.at[slot],
            device_id={"seq": seq, "dp": dp},
            device_id_type=MESH,
        )

    def own(self):
        return pltpu.make_async_copy(
            self.x_ref.at[lax.axis_index("seq"), lax.axis_index("dp")],
            self.out_ref.at[self.mine // self.lanes],
            self.own_sem,
        )

    def start(self):
        @pl.when(self.sender)
        def _():
            for hop in range(len(self.peers)):
                self.copy(hop, self.mine // self.lanes).start()
            self.own().start()

    def finish(self):
        for slot in range((len(self.peers) + 1) // self.lanes):

            @pl.when(self.lane + slot * self.lanes != self.mine)
            def _():
                self.copy(0, slot).wait_recv()

        @pl.when(self.sender)
        def _():
            for hop in range(len(self.peers)):
                self.copy(hop, self.mine // self.lanes).wait_send()
            self.own().wait()


def exchange_semaphores():
    count, lanes = lax.axis_size("seq") * lax.axis_size("dp"), lax.axis_size("tensor")
    return [
        pltpu.SemaphoreType.DMA((count - 1,)),
        pltpu.SemaphoreType.DMA((count // lanes,)),
        pltpu.SemaphoreType.DMA,
    ]


def turn(vectors, cosine, sine_part, direction):
    half = vectors.shape[-1] // 2
    low, high = vectors[:, :half], vectors[:, half:]
    return jnp.concatenate(
        [
            low * cosine - direction * high * sine_part,
            high * cosine + direction * low * sine_part,
        ],
        -1,
    )


def product(left, right, left_dim, right_dim):
    return lax.dot_general(
        left, right, (((left_dim,), (right_dim,)), ((), ())), preferred_element_type=jnp.float32
    )


def attend_kernel(
    width_q,
    proj_ref,
    cos_ref,
    sin_ref,
    cot_ref,
    block_ref,
    out_ref,
    blocks_ref,
    held,
    before,
    back_out,
    back_in,
    own_grad,
    kv_sems,
    back_sems,
    *exchange_sems,
):
    rows = proj_ref.shape[0]
    width_k = (proj_ref.shape[1] - width_q) // 2
    heads_k = width_k // HD
    group = width_q // width_k
    inv_scale = 1.0 / math.sqrt(HD)
    seqs, seq = lax.axis_size("seq"), lax.axis_index("seq")
    cosine, sine_part = cos_ref[...], sin_ref[...]
    for head in range(heads_k):
        low = head * HD
        at = slice(low, low + HD)
        keys = proj_ref[:, width_q + low : width_q + low + HD]
        held[:, at] = turn(keys, cosine, sine_part, 1.0).astype(jnp.bfloat16)
        values = proj_ref[:, width_q + width_k + low : width_q + width_k + low + HD]
        held[:, width_k + low : width_k + low + HD] = values.astype(jnp.bfloat16)
    _, peers = block_peers()
    greet((), [{"seq": other, "dp": far} for _, other, far in peers])
    ahead = pltpu.make_async_remote_copy(
        src_ref=held,
        dst_ref=before,
        send_sem=kv_sems.at[0],
        recv_sem=kv_sems.at[1],
        device_id={"seq": seq + 1},
        device_id_type=MESH,
    )
    behind = pltpu.make_async_remote_copy(
        src_ref=back_out,
        dst_ref=back_in,
        send_sem=back_sems.at[0],
        recv_sem=back_sems.at[1],
        device_id={"seq": seq - 1},
        device_id_type=MESH,
    )
    has_next, has_last = seq < seqs - 1, seq > 0

    @pl.when(has_next)
    def _():
        ahead.start()

    exchange = Exchange(block_ref, blocks_ref, *exchange_sems)
    exchange.start()

    queries = []
    for head in range(heads_k * group):
        part = proj_ref[:, head * HD : (head + 1) * HD]
        queries.append(turn(part, cosine, sine_part, 1.0).astype(jnp.bfloat16))

    @pl.when(has_last)
    def _():
        ahead.wait_recv()

    @pl.when(jnp.logical_not(has_last))
    def _():
        before[...] = jnp.zeros_like(before)

    query_at = lax.broadcasted_iota(jnp.int32, (rows, rows), 0)
    key_at = lax.broadcasted_iota(jnp.int32, (rows, rows), 1)
    masks = (
        (key_at > query_at + (rows - WINDOW)) & (seq * rows - rows + key_at >= 0),
        (key_at <= query_at) & (key_at > query_at - WINDOW),
    )
    for head in range(heads_k):
        at = slice(head * HD, (head + 1) * HD)
        at_value = slice(width_k + head * HD, width_k + (head + 1) * HD)
        sides = (before, held)
        key_grads, value_grads = [0.0, 0.0], [0.0, 0.0]
        for member in range(group):
            index = head * group + member
            query = queries[index]
            cot = cot_ref[:, index * HD : (index + 1) * HD]
            squashes, terms, slopes = [], [], []
            for side, mask in zip(sides, masks):
                squash = jnp.tanh(product(query, side[:, at], 1, 1) * inv_scale / SOFTCAP)
                squashes.append(squash)
                terms.append(jnp.where(mask, jnp.exp(SOFTCAP * squash), 0.0))
                slopes.append(product(cot, side[:, at_value], 1, 1))
            total = sum(jnp.sum(term, -1, keepdims=True) for term in terms)
            probs = [term / total for term in terms]
            delta = sum(
                jnp.sum(prob * slope, -1, keepdims=True) for prob, slope in zip(probs, slopes)
            )
            dquery = 0.0
            for which in range(2):
                prob, squash = probs[which], squashes[which]
                dlogits = (
                    prob * (slopes[which] - delta) * (1.0 - squash * squash) * inv_scale
                ).astype(jnp.bfloat16)
                dquery = dquery + product(dlogits, sides[which][:, at], 1, 0)
                key_grads[which] = key_grads[which] + product(dlogits, query, 0, 0)
                value_grads[which] = value_grads[which] + product(
                    prob.astype(jnp.bfloat16), cot, 0, 0
                )
            out_ref[:, index * HD : (index + 1) * HD] = turn(
                dquery, cosine, sine_part, -1.0
            ).astype(jnp.bfloat16)
        back_out[:, at] = key_grads[0].astype(jnp.bfloat16)
        back_out[:, at_value] = value_grads[0].astype(jnp.bfloat16)
        own_grad[:, at] = key_grads[1]
        own_grad[:, at_value] = value_grads[1]

    @pl.when(has_last)
    def _():
        behind.start()

    @pl.when(has_next)
    def _():
        behind.wait_recv()
        own_grad[...] += back_in[...].astype(jnp.float32)

    for head in range(heads_k):
        at = slice(head * HD, (head + 1) * HD)
        out_ref[:, width_q + head * HD : width_q + (head + 1) * HD] = turn(
            own_grad[:, at], cosine, sine_part, -1.0
        ).astype(jnp.bfloat16)
    out_ref[:, width_q + width_k :] = own_grad[:, width_k:].astype(jnp.bfloat16)

    @pl.when(has_next)
    def _():
        ahead.wait_send()

    @pl.when(has_last)
    def _():
        behind.wait_send()

    exchange.finish()


def attend_and_exchange(projected, cosine, sine_part, cotangent, blocks, collective_id):
    rows, width_q = cotangent.shape
    width_k = (projected.shape[1] - width_q) // 2
    return pl.pallas_call(
        functools.partial(attend_kernel, width_q),
        out_shape=(
            jax.ShapeDtypeStruct(projected.shape, jnp.bfloat16),
            jax.ShapeDtypeStruct(
                (blocks.shape[0] * blocks.shape[1] // lax.axis_size("tensor"),)
                + blocks.shape[2:],
                blocks.dtype,
            ),
        ),
        in_specs=[pl.BlockSpec(memory_space=pltpu.VMEM)] * 5,
        out_specs=(pl.BlockSpec(memory_space=pltpu.VMEM), pl.BlockSpec(memory_space=pl.ANY)),
        scratch_shapes=[
            pltpu.VMEM((rows, 2 * width_k), jnp.bfloat16),
            pltpu.VMEM((rows, 2 * width_k), jnp.bfloat16),
            pltpu.VMEM((rows, 2 * width_k), jnp.bfloat16),
            pltpu.VMEM((rows, 2 * width_k), jnp.bfloat16),
            pltpu.VMEM((rows, 2 * width_k), jnp.float32),
            pltpu.SemaphoreType.DMA((2,)),
            pltpu.SemaphoreType.DMA((2,)),
        ]
        + exchange_semaphores(),
        compiler_params=pltpu.CompilerParams(
            collective_id=collective_id, has_side_effects=True
        ),
    )(projected, cosine, sine_part, cotangent, blocks)


def total_kernel(x_ref, out_ref, held, send_sem, recv_sem, send_wide, recv_wide, own_sem):
    mine, peers = block_peers()
    lane = lax.axis_index("tensor")
    others = tensor_peers()
    own = pltpu.make_async_copy(x_ref, held.at[lane, mine], own_sem)
    own.start()
    greet(
        (),
        [{"seq": seq, "dp": dp} for _, seq, dp in peers] + [{"tensor": other} for other in others],
    )
    near = [
        pltpu.make_async_remote_copy(
            src_ref=x_ref,
            dst_ref=held.at[lane, mine],
            send_sem=send_sem.at[hop],
            recv_sem=recv_sem.at[mine],
            device_id={"seq": seq, "dp": dp},
            device_id_type=MESH,
        )
        for hop, (_, seq, dp) in enumerate(peers)
    ]
    for copy in near:
        copy.start()
    for index, seq, dp in peers:
        pltpu.make_async_remote_copy(
            src_ref=x_ref,
            dst_ref=held.at[lane, index],
            send_sem=send_sem.at[0],
            recv_sem=recv_sem.at[index],
            device_id={"seq": seq, "dp": dp},
            device_id_type=MESH,
        ).wait_recv()
    own.wait()
    far = [
        pltpu.make_async_remote_copy(
            src_ref=held.at[lane],
            dst_ref=held.at[lane],
            send_sem=send_wide.at[hop],
            recv_sem=recv_wide.at[hop],
            device_id={"tensor": other},
            device_id_type=MESH,
        )
        for hop, other in enumerate(others)
    ]
    for copy in far:
        copy.start()
    for copy in far:
        copy.wait()
    for copy in near:
        copy.wait_send()
    out_ref[...] = jnp.sum(held[...], (0, 1))


def total_of(x, collective_id):
    count, lanes = lax.axis_size("seq") * lax.axis_size("dp"), lax.axis_size("tensor")
    return pl.pallas_call(
        total_kernel,
        out_shape=jax.ShapeDtypeStruct(x.shape, x.dtype),
        in_specs=[pl.BlockSpec(memory_space=pltpu.VMEM)],
        out_specs=pl.BlockSpec(memory_space=pltpu.VMEM),
        scratch_shapes=[
            pltpu.VMEM((lanes, count) + x.shape, x.dtype),
            pltpu.SemaphoreType.DMA((count - 1,)),
            pltpu.SemaphoreType.DMA((count,)),
            pltpu.SemaphoreType.DMA((lanes - 1,)),
            pltpu.SemaphoreType.DMA((lanes - 1,)),
            pltpu.SemaphoreType.DMA,
        ],
        compiler_params=pltpu.CompilerParams(
            collective_id=collective_id, has_side_effects=True
        ),
    )(x)


def cut_of(rows):
    return max(16, rows // 7 // 16 * 16)


def gathered_local(inputs, w_query, w_key, w_value, norm_gain, attn_grad):
    widened = inputs[0].astype(jnp.float32)
    row_count = widened.shape[0]
    inverse_rms = lax.rsqrt(jnp.mean(widened * widened, -1) + EPSILON)
    normed = (widened * inverse_rms[:, None] * norm_gain[None, :]).astype(jnp.bfloat16)
    width_q = w_query.shape[1]
    width_k = w_key.shape[1]
    local_w = jnp.concatenate([w_query, w_key, w_value], 1)
    seqs, dps = lax.axis_size("seq"), lax.axis_size("dp")
    rows_w = local_w.shape[0]
    full_w = gather_blocks(local_w, cut_of(rows_w), ("seq", "dp"), 0)
    full_w = full_w.reshape(seqs * dps * rows_w, -1)
    projected = jnp.dot(normed, full_w, preferred_element_type=jnp.float32)
    start_row = lax.axis_index("seq") * row_count
    cosine, sine_part = angles(start_row + jnp.arange(row_count, dtype=jnp.int32), HD)
    d_out, passed = attend_and_exchange(
        projected,
        cosine[:, 0],
        sine_part[:, 0],
        attn_grad[0],
        normed.T.reshape(seqs, dps, rows_w, row_count),
        3,
    )
    dnormed = lax.dot_general(
        d_out, full_w, (((1,), (1,)), ((), ())), preferred_element_type=jnp.float32
    )
    inner = jnp.sum(widened * norm_gain[None, :] * dnormed, -1).reshape(-1, 128)
    cotangents, parts, inners, slabs = gather_and_scatter(
        d_out, dnormed.astype(jnp.bfloat16), inner, passed, cut_of(row_count), ("dp", "seq"), 2
    )
    grads = []
    lanes = lax.axis_size("tensor")
    for example in range(dps):
        grads.append(
            sum(
                jnp.dot(
                    slabs[(example * seqs + s) % lanes, (example * seqs + s) // lanes],
                    cotangents[example, s],
                    preferred_element_type=jnp.float32
                )
                for s in range(seqs)
            )
        )
    squares = jnp.stack([jnp.sum(grad * grad) for grad in grads])
    square_sum = total_of(jnp.broadcast_to(squares[:, None], (dps, 128)), 1)[:, 0]
    grad_rms = jnp.sqrt(square_sum / (D * (H + 2 * KVH) * HD) + EPSILON)
    factor = CLIP_BOUND / jnp.maximum(grad_rms, CLIP_BOUND)
    clipped = sum(factor[example] * grads[example] for example in range(dps))
    part_width = D // lax.axis_size("tensor")
    offset = lax.axis_index("tensor") * part_width
    part_grad = jnp.sum(parts.astype(jnp.float32), 0)
    gain_slab = lax.dynamic_slice_in_dim(norm_gain, offset, part_width, 0)
    input_slab = lax.dynamic_slice_in_dim(widened, offset, part_width, 1)
    scaled = gain_slab[None, :] * part_grad
    inner_sum = jnp.sum(inners, 0).reshape(row_count)
    mean_term = (inner_sum / D)[:, None]
    input_grad = (
        inverse_rms[:, None] * scaled
        - input_slab * (inverse_rms * inverse_rms * inverse_rms)[:, None] * mean_term
    )
    return (
        clipped[:, :width_q],
        clipped[:, width_q : width_q + width_k],
        clipped[:, width_q + width_k :],
        input_grad.astype(jnp.bfloat16)[None],
    )


def attend_alone_kernel(
    width_q,
    proj_ref,
    cos_ref,
    sin_ref,
    cot_ref,
    out_ref,
    inner_ref,
    held,
    before,
    back_out,
    back_in,
    own_grad,
    kv_sems,
    back_sems,
):
    rows = proj_ref.shape[0]
    width_k = (proj_ref.shape[1] - width_q) // 2
    heads_k = width_k // HD
    group = width_q // width_k
    inv_scale = 1.0 / math.sqrt(HD)
    seqs, seq = lax.axis_size("seq"), lax.axis_index("seq")
    cosine, sine_part = cos_ref[...], sin_ref[...]
    for head in range(heads_k):
        low = head * HD
        at = slice(low, low + HD)
        keys = proj_ref[:, width_q + low : width_q + low + HD]
        held[:, at] = turn(keys, cosine, sine_part, 1.0).astype(jnp.bfloat16)
        values = proj_ref[:, width_q + width_k + low : width_q + width_k + low + HD]
        held[:, width_k + low : width_k + low + HD] = values.astype(jnp.bfloat16)
    greet(("seq",))
    ahead = pltpu.make_async_remote_copy(
        src_ref=held,
        dst_ref=before,
        send_sem=kv_sems.at[0],
        recv_sem=kv_sems.at[1],
        device_id={"seq": seq + 1},
        device_id_type=MESH,
    )
    behind = pltpu.make_async_remote_copy(
        src_ref=back_out,
        dst_ref=back_in,
        send_sem=back_sems.at[0],
        recv_sem=back_sems.at[1],
        device_id={"seq": seq - 1},
        device_id_type=MESH,
    )
    has_next, has_last = seq < seqs - 1, seq > 0

    @pl.when(has_next)
    def _():
        ahead.start()

    queries = []
    for head in range(heads_k * group):
        part = proj_ref[:, head * HD : (head + 1) * HD]
        queries.append(turn(part, cosine, sine_part, 1.0).astype(jnp.bfloat16))

    @pl.when(has_last)
    def _():
        ahead.wait_recv()

    @pl.when(jnp.logical_not(has_last))
    def _():
        before[...] = jnp.zeros_like(before)

    query_at = lax.broadcasted_iota(jnp.int32, (rows, rows), 0)
    key_at = lax.broadcasted_iota(jnp.int32, (rows, rows), 1)
    masks = (
        (key_at > query_at + (rows - WINDOW)) & (seq * rows - rows + key_at >= 0),
        (key_at <= query_at) & (key_at > query_at - WINDOW),
    )
    for head in range(heads_k):
        at = slice(head * HD, (head + 1) * HD)
        at_value = slice(width_k + head * HD, width_k + (head + 1) * HD)
        sides = (before, held)
        key_grads, value_grads = [0.0, 0.0], [0.0, 0.0]
        for member in range(group):
            index = head * group + member
            query = queries[index]
            cot = cot_ref[:, index * HD : (index + 1) * HD]
            squashes, terms, slopes = [], [], []
            for side, mask in zip(sides, masks):
                squash = jnp.tanh(product(query, side[:, at], 1, 1) * inv_scale / SOFTCAP)
                squashes.append(squash)
                terms.append(jnp.where(mask, jnp.exp(SOFTCAP * squash), 0.0))
                slopes.append(product(cot, side[:, at_value], 1, 1))
            total = sum(jnp.sum(term, -1, keepdims=True) for term in terms)
            probs = [term / total for term in terms]
            delta = sum(
                jnp.sum(prob * slope, -1, keepdims=True) for prob, slope in zip(probs, slopes)
            )
            dquery = 0.0
            for which in range(2):
                prob, squash = probs[which], squashes[which]
                dlogits = (
                    prob * (slopes[which] - delta) * (1.0 - squash * squash) * inv_scale
                ).astype(jnp.bfloat16)
                dquery = dquery + product(dlogits, sides[which][:, at], 1, 0)
                key_grads[which] = key_grads[which] + product(dlogits, query, 0, 0)
                value_grads[which] = value_grads[which] + product(
                    prob.astype(jnp.bfloat16), cot, 0, 0
                )
            out_ref[:, index * HD : (index + 1) * HD] = turn(
                dquery, cosine, sine_part, -1.0
            ).astype(jnp.bfloat16)
        back_out[:, at] = key_grads[0].astype(jnp.bfloat16)
        back_out[:, at_value] = value_grads[0].astype(jnp.bfloat16)
        own_grad[:, at] = key_grads[1]
        own_grad[:, at_value] = value_grads[1]

    @pl.when(has_last)
    def _():
        behind.start()

    @pl.when(has_next)
    def _():
        behind.wait_recv()
        own_grad[...] += back_in[...].astype(jnp.float32)

    for head in range(heads_k):
        at = slice(head * HD, (head + 1) * HD)
        out_ref[:, width_q + head * HD : width_q + (head + 1) * HD] = turn(
            own_grad[:, at], cosine, sine_part, -1.0
        ).astype(jnp.bfloat16)
    out_ref[:, width_q + width_k :] = own_grad[:, width_k:].astype(jnp.bfloat16)

    @pl.when(has_next)
    def _():
        ahead.wait_send()

    @pl.when(has_last)
    def _():
        behind.wait_send()

    inner = 0.0
    for low in range(0, out_ref.shape[1], 128):
        at = slice(low, low + 128)
        inner = inner + out_ref[:, at].astype(jnp.float32) * proj_ref[:, at]
    inner = jnp.broadcast_to(jnp.sum(inner, -1, keepdims=True), (rows, 128))
    inner_ref[...] = inner.T[:8]


def attend_alone(projected, cosine, sine_part, cotangent, collective_id):
    rows, width_q = cotangent.shape
    width_k = (projected.shape[1] - width_q) // 2
    return pl.pallas_call(
        functools.partial(attend_alone_kernel, width_q),
        out_shape=(
            jax.ShapeDtypeStruct(projected.shape, jnp.bfloat16),
            jax.ShapeDtypeStruct((8, rows), jnp.float32),
        ),
        in_specs=[pl.BlockSpec(memory_space=pltpu.VMEM)] * 4,
        out_specs=(pl.BlockSpec(memory_space=pltpu.VMEM),) * 2,
        scratch_shapes=[
            pltpu.VMEM((rows, 2 * width_k), jnp.bfloat16),
            pltpu.VMEM((rows, 2 * width_k), jnp.bfloat16),
            pltpu.VMEM((rows, 2 * width_k), jnp.bfloat16),
            pltpu.VMEM((rows, 2 * width_k), jnp.bfloat16),
            pltpu.VMEM((rows, 2 * width_k), jnp.float32),
            pltpu.SemaphoreType.DMA((2,)),
            pltpu.SemaphoreType.DMA((2,)),
        ],
        compiler_params=pltpu.CompilerParams(
            collective_id=collective_id, has_side_effects=True
        ),
    )(projected, cosine, sine_part, cotangent)


def others_of(axis):
    count, me = lax.axis_size(axis), lax.axis_index(axis)
    return [lax.rem(me + hop, count) for hop in range(1, count)]


def signal_all(peers):
    barrier = pltpu.get_barrier_semaphore()
    for peer in peers:
        pl.semaphore_signal(barrier, inc=1, device_id=peer, device_id_type=MESH)
    return barrier


def remote(src, dst, send_sem, recv_sem, device):
    return pltpu.make_async_remote_copy(
        src_ref=src,
        dst_ref=dst,
        send_sem=send_sem,
        recv_sem=recv_sem,
        device_id=device,
        device_id_type=MESH,
    )


def line(axis, far_first):
    count, me = lax.axis_size(axis), lax.axis_index(axis)
    order = range(count - 1, 0, -1) if far_first else range(1, count)
    found = []
    for hop in order:
        for which, step in enumerate((-1, 1)):
            at = me + step * hop
            found.append((2 * hop - 2 + which, step, at, (at >= 0) & (at < count)))
    return found


def halvings(block):
    lanes, lane = lax.axis_size("tensor"), lax.axis_index("tensor")
    stages = lanes.bit_length() - 1
    bits = [lax.rem(lane // (1 << stage), 2) for stage in range(stages)]
    return bits, [block >> stage for stage in range(stages + 1)]


def lane_start(lane, block):
    stages = lax.axis_size("tensor").bit_length() - 1
    return sum(((lane >> stage) & 1) * (block >> (stage + 1)) for stage in range(stages))


def partner(bits, stage):
    return {"tensor": lax.axis_index("tensor") + (1 - 2 * bits[stage]) * (1 << stage)}


def project_kernel(
    x_ref,
    gain_ref,
    wq_ref,
    wk_ref,
    wv_ref,
    proj_ref,
    w_ref,
    slabs_ref,
    rms_ref,
    turned,
    every,
    natural,
    acc,
    sent,
    got,
    w_send,
    w_recv,
    own_sem,
    x_send,
    x_recv,
    f_send,
    f_recv,
    r_send,
    r_recv,
    s_send,
    s_recv,
):
    seqs, dps, lanes = (lax.axis_size(axis) for axis in ("seq", "dp", "tensor"))
    seq, dp, lane = (lax.axis_index(axis) for axis in ("seq", "dp", "tensor"))
    rows, features = x_ref.shape
    block = wq_ref.shape[0]
    bits, sizes = halvings(block)
    stages = len(bits)

    def region(stage):
        start = sum(bits[level] * sizes[level + 1] for level in range(stage + 1))
        return pl.ds(pl.multiple_of(start, 16), sizes[stage + 1])

    mine = region(stages - 1)
    peers = [{axis: other} for axis in ("seq", "dp", "tensor") for other in others_of(axis)]
    barrier = signal_all(peers)
    squares = jnp.zeros((rows, 128), jnp.float32)
    for low in range(0, features, 128):
        part = x_ref[:, low : low + 128].astype(jnp.float32)
        squares = squares + part * part
    inverse = lax.rsqrt(jnp.sum(squares, -1, keepdims=True) / features + EPSILON)
    rms_ref[...] = jnp.broadcast_to(inverse, rms_ref.shape)
    pl.semaphore_wait(barrier, len(peers))

    chunks, base = [], 0
    for ref in (wq_ref, wk_ref, wv_ref):
        chunks.append([(ref, low, base + low) for low in range(0, ref.shape[1], HD)])
        base = base + ref.shape[1]
    chunks = chunks[1] + chunks[2] + chunks[0]

    def w_copy(index, hop, other):
        ref, low, to = chunks[index]
        return remote(
            ref.at[:, low : low + HD],
            w_ref.at[seq, :, to : to + HD],
            w_send.at[hop, index],
            w_recv.at[seq, index],
            {"seq": other},
        )

    owns = []
    for index, (ref, low, to) in enumerate(chunks):
        owns.append(
            pltpu.make_async_copy(
                ref.at[:, low : low + HD], w_ref.at[seq, :, to : to + HD], own_sem.at[index]
            )
        )
        owns[-1].start()
        for hop, other in enumerate(others_of("seq")):
            w_copy(index, hop, other).start()

    for low in range(0, features, 128):
        part = x_ref[:, low : low + 128].astype(jnp.float32)
        part = (part * inverse * gain_ref[low : low + 128][None, :]).astype(jnp.bfloat16).T
        at = low
        while at < low + 128:
            index = at // block
            end = min(low + 128, (index + 1) * block)
            turned[index // dps, index % dps, at - index * block : end - index * block, :] = part[
                at - low : end - low
            ]
            at = end

    def x_copy(other):
        return remote(
            turned.at[:, other, mine],
            every.at[dp, :, mine],
            x_send.at[other],
            x_recv.at[dp],
            {"dp": other},
        )

    own_x = pltpu.make_async_copy(turned.at[:, dp], every.at[dp], own_sem.at[len(chunks)])
    own_x.start()
    for _, _, other, held in line("dp", False):

        @pl.when(held)
        def _():
            x_copy(other).start()

    def f_copy(stage, source):
        part = every.at[source, :, region(stage)]
        return remote(
            part, part, f_send.at[stage, source], f_recv.at[stage, source], partner(bits, stage)
        )

    def x_arrival(source):
        part = every.at[source, :, mine]
        remote(part, part, x_send.at[source], x_recv.at[source], {"dp": source}).wait_recv()

    def partial(source, index):
        _, _, to = chunks[index]
        weights = w_ref[:, :, to : to + HD].reshape(seqs * block, HD)
        return product(natural[source], weights, 1, 0)

    def turn_back(source):
        natural[source] = every[source].reshape(seqs * block, rows).T

    def r_copy(step, index, which, target):
        way = 0 if step == -1 else 1
        return remote(
            sent.at[index, which],
            got.at[way, index, target],
            r_send.at[index, which],
            r_recv.at[way, index, target],
            {"dp": dp + step},
        )

    def upstream(step):
        return dp < dps - 1 if step == -1 else dp > 0

    def r_arrival(step, index, target):
        way = 0 if step == -1 else 1
        remote(
            got.at[way, index, target],
            got.at[way, index, target],
            r_send.at[index, 0],
            r_recv.at[way, index, target],
            {"dp": dp},
        ).wait_recv()
        acc[...] += got[way, index, target].astype(jnp.float32)

    def finish_chunk(index):
        _, _, to = chunks[index]
        acc[...] = partial(dp, index)
        for step in (-1, 1):

            @pl.when(upstream(step))
            def _():
                r_arrival(step, index, dp)

        proj_ref[:, to : to + HD] = acc[...]

    slab_own = pltpu.make_async_copy(
        every.at[:, seq], slabs_ref.at[seq], own_sem.at[len(chunks) + 1]
    )

    def s_copy(hop, other):
        return remote(
            every.at[:, other], slabs_ref.at[seq], s_send.at[hop], s_recv.at[seq], {"seq": other}
        )

    def weights_ready(index):
        owns[index].wait()
        for other in others_of("seq"):
            _, _, to = chunks[index]
            remote(
                w_ref.at[other, :, to : to + HD],
                w_ref.at[other, :, to : to + HD],
                w_send.at[0, index],
                w_recv.at[other, index],
                {"seq": other},
            ).wait_recv()

    def pass_on(which, step, index, target):
        acc[...] = partial(target, index)

        @pl.when(upstream(step))
        def _():
            r_arrival(step, index, target)

        sent[index, which] = acc[...].astype(jnp.bfloat16)
        r_copy(step, index, which, target).start()

    def phase(number, which, step, source):
        if number == 0:
            x_arrival(source)
        else:
            f_copy(stages - number, source).wait_recv()
        if number < stages:
            f_copy(stages - 1 - number, source).start()
        else:
            turn_back(source)

            @pl.when(jnp.logical_not(upstream(step)))
            def _():
                pass_on(which, step, 0, source)

    nearest = line("dp", False)
    for tick in range(dps - 1 + stages):
        if tick == stages:
            weights_ready(0)
        for number in range(stages + 1):
            hop = tick - number
            if 0 <= hop < dps - 1:
                for which, step, source, held in nearest[2 * hop : 2 * hop + 2]:

                    @pl.when(held)
                    def _():
                        phase(number, which, step, source)

    for which, step, target, held in line("dp", True):

        @pl.when(held & upstream(step))
        def _():
            pass_on(which, step, 0, target)

    own_x.wait()
    turn_back(dp)
    slab_own.start()
    for hop, other in enumerate(others_of("seq")):
        s_copy(hop, other).start()
    for index in range(1, len(chunks)):
        weights_ready(index)
        for which, step, target, held in line("dp", True):

            @pl.when(held)
            def _():
                pass_on(which, step, index, target)

        finish_chunk(index - 1)
    finish_chunk(len(chunks) - 1)

    slab_own.wait()
    for hop, other in enumerate(others_of("seq")):
        s_copy(hop, other).wait_send()
        remote(
            every.at[:, other], slabs_ref.at[other], s_send.at[hop], s_recv.at[other], {"seq": other}
        ).wait_recv()
        for index in range(len(chunks)):
            w_copy(index, hop, other).wait_send()
    for which, step, target, held in line("dp", True):

        @pl.when(held)
        def _():
            x_copy(target).wait_send()
            for stage in range(stages):
                f_copy(stage, target).wait_send()
            for index in range(len(chunks)):
                r_copy(step, index, which, target).wait_send()


def project(x, gain, w_query, w_key, w_value, collective_id):
    seqs, dps, lanes = (lax.axis_size(axis) for axis in ("seq", "dp", "tensor"))
    rows, features = x.shape
    block = w_query.shape[0]
    width = w_query.shape[1] + w_key.shape[1] + w_value.shape[1]
    count = width // HD
    hops, stages = 2 * (dps - 1), lanes.bit_length() - 1
    vmem = pl.BlockSpec(memory_space=pltpu.VMEM)
    dma = pltpu.SemaphoreType.DMA
    return pl.pallas_call(
        project_kernel,
        out_shape=(
            jax.ShapeDtypeStruct((rows, width), jnp.float32),
            jax.ShapeDtypeStruct((seqs, block, width), jnp.bfloat16),
            jax.ShapeDtypeStruct((seqs, dps, block, rows), jnp.bfloat16),
            jax.ShapeDtypeStruct((rows, 128), jnp.float32),
        ),
        in_specs=[vmem, vmem] + [pl.BlockSpec(memory_space=pl.ANY)] * 3,
        out_specs=(vmem,) * 4,
        scratch_shapes=[
            pltpu.VMEM((seqs, dps, block, rows), jnp.bfloat16),
            pltpu.VMEM((dps, seqs, block, rows), jnp.bfloat16),
            pltpu.VMEM((dps, rows, seqs * block), jnp.bfloat16),
            pltpu.VMEM((rows, HD), jnp.float32),
            pltpu.VMEM((count, hops, rows, HD), jnp.bfloat16),
            pltpu.VMEM((2, count, dps, rows, HD), jnp.bfloat16),
            dma((seqs - 1, count)),
            dma((seqs, count)),
            dma((count + 2,)),
            dma((dps,)),
            dma((dps,)),
            dma((stages, dps)),
            dma((stages, dps)),
            dma((count, hops)),
            dma((2, count, dps)),
            dma((seqs - 1,)),
            dma((seqs,)),
        ],
        compiler_params=pltpu.CompilerParams(
            collective_id=collective_id, has_side_effects=True
        ),
    )(x, gain, w_query, w_key, w_value)


def split_rows(rows):
    return max(16, rows // 6 // 16 * 16)


def backward_kernel(
    cut,
    d_out_ref,
    w_ref,
    slabs_ref,
    inner_ref,
    rms_ref,
    x_ref,
    gain_ref,
    gq_ref,
    gk_ref,
    gv_ref,
    out_ref,
    every,
    grads,
    final,
    inners,
    squares,
    small,
    held_sums,
    x_slab,
    *rest,
):
    seqs, dps, lanes = (lax.axis_size(axis) for axis in ("seq", "dp", "tensor"))
    seq, dp, lane = (lax.axis_index(axis) for axis in ("seq", "dp", "tensor"))
    stages = lanes.bit_length() - 1
    parts, rest = rest[: stages + 1], rest[stages + 1 :]
    arrived, rest = rest[:stages], rest[stages:]
    (g_send, g_recv, own_sem, p_send, p_recv, z_send, z_recv, i_send, i_recv) = rest[:9]
    t_send, t_recv, u_send, u_recv = rest[9:]
    rows, width = d_out_ref.shape
    block = w_ref.shape[1]
    per_slab = seqs * dps // lanes
    part_width = per_slab * block
    column_blocks = width // HD

    near = [{"dp": far, "tensor": other} for far in others_of("dp") for other in others_of("tensor")]
    near = near + [{"tensor": other} for other in others_of("tensor")]
    mine, blocks = block_peers()
    near = near + [{"seq": other, "dp": far} for _, other, far in blocks]
    barrier = signal_all(near)
    owns = [
        pltpu.make_async_copy(d_out_ref, every.at[dp, seq], own_sem.at[0]),
        pltpu.make_async_copy(
            x_ref.at[:, pl.ds(pl.multiple_of(lane * part_width, 128), part_width)],
            x_slab,
            own_sem.at[1],
        ),
        pltpu.make_async_copy(inner_ref, inners.at[lane], own_sem.at[2]),
    ]
    for own in owns:
        own.start()
    pl.semaphore_wait(barrier, len(near))

    order = ("dp", "seq")
    by_seq = LineGather(order, 0, "seq", "dp", 0, cut, d_out_ref, every, g_send, g_recv)
    by_dp = LineGather(order, 1, "dp", "seq", cut, rows, d_out_ref, every, g_send, g_recv)
    me = {"seq": seq, "dp": dp}
    here = jnp.bool_(True)
    for gather, axis in ((by_dp, "dp"), (by_dp, "seq"), (by_seq, "seq"), (by_seq, "dp")):
        for step in (1, -1):
            gather.send(dict(me), axis, step, here, True)
    inner_copies = [
        remote(inner_ref, inners.at[lane], i_send.at[hop], i_recv.at[lane], {"tensor": other})
        for hop, other in enumerate(others_of("tensor"))
    ]
    for copy in inner_copies:
        copy.start()

    def weight_grad(at, first):
        def column(index, carry):
            columns = pl.ds(pl.multiple_of(index * HD, HD), HD)
            term = product(slabs_ref[at["seq"], at["dp"]], every[at["dp"], at["seq"], :, columns], 1, 0)
            if first:
                grads[at["dp"], :, columns] = term
            else:
                grads[at["dp"], :, columns] = grads[at["dp"], :, columns] + term
            return carry

        lax.fori_loop(0, column_blocks, column, 0)

    def square_sum(example):
        def some(index, total):
            group = grads[example, pl.ds(pl.multiple_of(index * 16, 16), 16), :]
            group = group * group
            group = group[:8] + group[8:]
            for low in range(0, width, 128):
                total = total + group[:, low : low + 128]
            return total

        total = lax.fori_loop(0, block // 16, some, jnp.zeros((8, 128), jnp.float32))
        squares[example] = total

    bits, sizes = halvings(block)
    start = sum(bits[stage] * sizes[stage + 1] for stage in range(stages))

    def half(stage, bit):
        return pl.ds(pl.multiple_of(bit * sizes[stage + 1], 16), sizes[stage + 1])

    def p_copy(stage, example):
        return remote(
            parts[stage].at[example, :, half(stage, 1 - bits[stage])],
            arrived[stage].at[example],
            p_send.at[stage, example],
            p_recv.at[stage, example],
            partner(bits, stage),
        )

    def z_target(part):
        index = part * dps + dp
        return index // per_slab, lax.rem(index, per_slab)

    def z_copy(example, part):
        to, slot = z_target(part)
        return remote(
            parts[stages].at[example, part],
            final.at[slot, pl.ds(pl.multiple_of(start, 16), sizes[stages])],
            z_send.at[example, part],
            z_recv.at[slot, lane],
            {"tensor": to, "dp": example},
        )

    def z_own(example, part):
        _, slot = z_target(part)
        return pltpu.make_async_copy(
            parts[stages].at[example, part],
            final.at[slot, pl.ds(pl.multiple_of(start, 16), sizes[stages])],
            z_recv.at[slot, lane],
        )

    def z_is_own(example, part):
        to, _ = z_target(part)
        return (to == lane) & (example == dp)

    def advance(stage, example):
        if stage == 0:
            for part in range(seqs):
                parts[0][example, part] = product(
                    w_ref[part], every[example, seq], 1, 1
                ).astype(jnp.bfloat16)
        else:
            p_copy(stage - 1, example).wait_recv()
            kept = parts[stage - 1][example, :, half(stage - 1, bits[stage - 1])]
            added = arrived[stage - 1][example]
            parts[stage][example] = (
                kept.astype(jnp.float32) + added.astype(jnp.float32)
            ).astype(jnp.bfloat16)
        if stage < stages:
            p_copy(stage, example).start()
        else:
            for part in range(seqs):

                @pl.when(z_is_own(example, part))
                def _():
                    z_own(example, part).start()

                @pl.when(jnp.logical_not(z_is_own(example, part)))
                def _():
                    z_copy(example, part).start()

    groups = [[(dp, None)]] + [
        [
            (dp - step * hop, (dp - step * hop >= 0) & (dp - step * hop < dps))
            for step in (1, -1)
        ]
        for hop in range(1, dps)
    ]

    def each(hop, action):
        for example, held in groups[hop]:
            if held is None:
                action(example)
            else:

                @pl.when(held)
                def _():
                    action(example)

    def spread(hop):
        column = []
        for example, held in groups[hop]:
            column.append(({**me, "dp": example}, here if held is None else held))
        found = []
        for base, held_base in column:
            for far in range(1, seqs):
                for step in (1, -1):
                    at = {**base, "seq": seq - step * far}
                    held = held_base & by_dp.inside("seq", at["seq"])
                    by_dp.receive(at, held)
                    by_dp.send(at, "seq", step, held)
                    found.append((at, held))
        for at, held in found:

            @pl.when(held)
            def _():
                weight_grad(at, False)

        each(hop, square_sum)

    base_columns = [(dict(me), here)]
    for hop in range(1, seqs):
        for step in (1, -1):
            at = {**me, "seq": seq - step * hop}
            held = by_seq.inside("seq", at["seq"])
            by_seq.receive(at, held)
            by_seq.send(at, "seq", step, held)
            for way in (1, -1):
                by_seq.send(at, "dp", way, held)
            base_columns.append((at, held))
    owns[0].wait()
    each(0, functools.partial(advance, 0))
    each(0, lambda example: weight_grad({**me, "dp": example}, True))
    for hop in range(1, dps):
        for step in (1, -1):
            at = {**me, "dp": dp - step * hop}
            held = by_dp.inside("dp", at["dp"])
            by_dp.receive(at, held)
            by_dp.send(at, "dp", step, held)
            for way in (1, -1):
                by_dp.send(at, "seq", way, held)
        for base, held_base in base_columns:
            for step in (1, -1):
                at = {**base, "dp": dp - step * hop}
                held = held_base & by_seq.inside("dp", at["dp"])
                by_seq.receive(at, held)
                by_seq.send(at, "dp", step, held)
        each(hop, functools.partial(advance, 0))
        for stage in range(1, stages + 1):
            if 0 <= hop - stage:
                each(hop - stage, functools.partial(advance, stage))
        each(hop, lambda example: weight_grad({**me, "dp": example}, True))
        spread(hop - 1)
    for late in range(1, stages + 1):
        for stage in range(late, stages + 1):
            if 0 <= dps - 1 + late - stage < dps:
                each(dps - 1 + late - stage, functools.partial(advance, stage))
        if late == 1:
            spread(dps - 1)
            for example in range(dps):
                small[example : example + 1, :] = jnp.sum(squares[example], 0, keepdims=True)
            own_sum = pltpu.make_async_copy(small, held_sums.at[lane, mine], own_sem.at[3])
            own_sum.start()
            sums = [
                remote(
                    small,
                    held_sums.at[lane, mine],
                    t_send.at[hop],
                    t_recv.at[mine],
                    {"seq": other, "dp": far},
                )
                for hop, (_, other, far) in enumerate(blocks)
            ]
            for copy in sums:
                copy.start()

    for hop, (index, other, far) in enumerate(blocks):
        remote(
            small,
            held_sums.at[lane, index],
            t_send.at[hop],
            t_recv.at[index],
            {"seq": other, "dp": far},
        ).wait_recv()
    own_sum.wait()
    wide = [
        remote(
            held_sums.at[lane],
            held_sums.at[lane],
            u_send.at[hop],
            u_recv.at[lane],
            {"tensor": other},
        )
        for hop, other in enumerate(others_of("tensor"))
    ]
    for copy in wide:
        copy.start()

    owns[1].wait()
    owns[2].wait()
    for hop, other in enumerate(others_of("tensor")):
        remote(
            inner_ref, inners.at[other], i_send.at[hop], i_recv.at[other], {"tensor": other}
        ).wait_recv()
    total = inners[0]
    for other in range(1, lanes):
        total = total + inners[other]
    total = jnp.broadcast_to(total[:1], (128, rows)).T
    inverse = rms_ref[...]
    mean = total * inverse * inverse / x_ref.shape[1]
    for slot in range(per_slab):
        for other in range(lanes):
            turn_start = lane_start(other, block)
            piece = final.at[slot, turn_start : turn_start + sizes[stages]]
            remote(
                piece, piece, z_send.at[0, 0], z_recv.at[slot, other], {"tensor": lane}
            ).wait_recv()
    for low in range(0, part_width, 128):
        pieces = []
        at = low
        while at < low + 128:
            slot = at // block
            end = min(low + 128, (slot + 1) * block)
            pieces.append(final[slot, at - slot * block : end - slot * block, :])
            at = end
        part = pieces[0] if len(pieces) == 1 else jnp.concatenate(pieces, 0)
        part = part.astype(jnp.float32).T
        gain = gain_ref[pl.ds(pl.multiple_of(lane * part_width + low, 128), 128)][None, :]
        scaled = part * gain
        out_ref[:, low : low + 128] = (
            inverse * scaled - x_slab[:, low : low + 128].astype(jnp.float32) * mean
        ).astype(jnp.bfloat16)

    for hop, other in enumerate(others_of("tensor")):
        remote(
            held_sums.at[other],
            held_sums.at[other],
            u_send.at[hop],
            u_recv.at[other],
            {"tensor": other},
        ).wait_recv()
    square = jnp.sum(jnp.sum(held_sums[...], (0, 1)), -1, keepdims=True)
    grad_rms = jnp.sqrt(square / (D * (H + 2 * KVH) * HD) + EPSILON)
    factor = CLIP_BOUND / jnp.maximum(grad_rms, CLIP_BOUND)
    base = 0
    for ref in (gq_ref, gk_ref, gv_ref):
        for low in range(0, ref.shape[1], 128):
            clipped = factor[0:1] * grads[0, :, base + low : base + low + 128]
            for example in range(1, dps):
                clipped = clipped + factor[example : example + 1] * (
                    grads[example, :, base + low : base + low + 128]
                )
            ref[:, low : low + 128] = clipped
        base = base + ref.shape[1]

    by_seq.finish()
    by_dp.finish()
    for copy in inner_copies + sums + wide:
        copy.wait_send()

    def drain(example):
        for stage in range(stages):
            p_copy(stage, example).wait_send()
        for part in range(seqs):

            @pl.when(jnp.logical_not(z_is_own(example, part)))
            def _():
                z_copy(example, part).wait_send()

    for hop in range(dps):
        each(hop, drain)


def backward(d_out, weights, slabs, inner, rms, x, gain, widths, collective_id):
    seqs, dps, lanes = (lax.axis_size(axis) for axis in ("seq", "dp", "tensor"))
    rows, width = d_out.shape
    block = weights.shape[1]
    features = x.shape[1]
    stages = lanes.bit_length() - 1
    per_slab = seqs * dps // lanes
    vmem = pl.BlockSpec(memory_space=pltpu.VMEM)
    dma = pltpu.SemaphoreType.DMA
    count = seqs * dps
    return pl.pallas_call(
        functools.partial(backward_kernel, split_rows(rows)),
        out_shape=tuple(jax.ShapeDtypeStruct((block, size), jnp.float32) for size in widths)
        + (jax.ShapeDtypeStruct((rows, features // lanes), jnp.bfloat16),),
        in_specs=[vmem] * 5 + [pl.BlockSpec(memory_space=pl.ANY), vmem],
        out_specs=(vmem,) * 4,
        scratch_shapes=[
            pltpu.VMEM((dps, seqs, rows, width), jnp.bfloat16),
            pltpu.VMEM((dps, block, width), jnp.float32),
            pltpu.VMEM((per_slab, block, rows), jnp.bfloat16),
            pltpu.VMEM((lanes,) + inner.shape, jnp.float32),
            pltpu.VMEM((dps, 8, 128), jnp.float32),
            pltpu.VMEM((dps, 128), jnp.float32),
            pltpu.VMEM((lanes, count, dps, 128), jnp.float32),
            pltpu.VMEM((rows, features // lanes), jnp.bfloat16),
        ]
        + [
            pltpu.VMEM((dps, seqs, block >> stage, rows), jnp.bfloat16)
            for stage in range(stages + 1)
        ]
        + [
            pltpu.VMEM((dps, seqs, block >> (stage + 1), rows), jnp.bfloat16)
            for stage in range(stages)
        ]
        + [
            dma((2, 4, seqs, dps)),
            dma((2, seqs, dps)),
            dma((4,)),
            dma((stages, dps)),
            dma((stages, dps)),
            dma((dps, seqs)),
            dma((per_slab, lanes)),
            dma((lanes - 1,)),
            dma((lanes,)),
            dma((count - 1,)),
            dma((count,)),
            dma((lanes - 1,)),
            dma((lanes,)),
        ],
        compiler_params=pltpu.CompilerParams(
            collective_id=collective_id, has_side_effects=True
        ),
    )(d_out, weights, slabs, inner, rms, x, gain)


def split_local(inputs, w_query, w_key, w_value, norm_gain, attn_grad):
    x, gain = inputs[0], norm_gain
    rows = x.shape[0]
    projected, weights, slabs, rms = project(x, gain, w_query, w_key, w_value, 0)
    start_row = lax.axis_index("seq") * rows
    cosine, sine_part = angles(start_row + jnp.arange(rows, dtype=jnp.int32), HD)
    d_out, inner = attend_alone(projected, cosine[:, 0], sine_part[:, 0], attn_grad[0], 3)
    widths = (w_query.shape[1], w_key.shape[1], w_value.shape[1])
    grad_query, grad_key, grad_value, input_grad = backward(
        d_out, weights, slabs, inner, rms, x, gain, widths, 2
    )
    return grad_query, grad_key, grad_value, input_grad[None]


def local(*args):
    inputs, w_query = args[:2]
    seqs, dps, lanes = (lax.axis_size(axis) for axis in ("seq", "dp", "tensor"))
    block = w_query.shape[0]
    aligned = block % (16 * lanes) == 0 and inputs.shape[1] % 128 == 0
    aligned = aligned and (block * seqs * dps // lanes) % 128 == 0
    even = lanes & (lanes - 1) == 0 and seqs * dps % lanes == 0
    if aligned and even and min(seqs, dps, lanes) > 1:
        return split_local(*args)
    return gathered_local(*args)


def solution(mesh):
    return jax.shard_map(
        local,
        mesh=mesh,
        in_specs=(
            P("dp", "seq", None),
            P(("seq", "dp"), "tensor"),
            P(("seq", "dp"), "tensor"),
            P(("seq", "dp"), "tensor"),
            P(),
            P("dp", "seq", "tensor"),
        ),
        out_specs=(
            P(("seq", "dp"), "tensor"),
            P(("seq", "dp"), "tensor"),
            P(("seq", "dp"), "tensor"),
            P("dp", "seq", "tensor"),
        ),
        check_vma=False,
    )
```
